32 devices in a mesh: groups: 2 (over y), grid: 4 (over z), mesh: 2 (over x), sub: 2 (over core).
Axes of the slice: x: 2, y: 2, z: 4, core: 2. Of those that a mesh axis runs over, the one named last changes fastest.
Arguments:
- grid_feat: bfloat16 [8192, 256], P(('groups', 'grid')), parts along dimension 0, may hold values from -6 to 6
- mesh_state: bfloat16 [3072, 1024], P(('groups', 'grid'), ('mesh', 'sub')), parts along dimension 0, may hold values from -6 to 6
- embed_weight: bfloat16 [256, 1024], P(None, ('mesh', 'sub')), may hold values from -0.375 to 0.375
- embed_gain: float32 [1024], P(('mesh', 'sub')), may hold values from 0.25 to 1.75
- enc_send_weight: bfloat16 [1024, 1024], P(None, ('mesh', 'sub')), may hold values from -0.1875 to 0.1875
- enc_recv_weight: bfloat16 [1024, 1024], P(None, ('mesh', 'sub')), may hold values from -0.1875 to 0.1875
- enc_bias: float32 [1024], P(('mesh', 'sub')), may hold values from -3 to 3
- enc_out_weight: bfloat16 [1024, 1024], P(None, ('mesh', 'sub')), may hold values from -0.1875 to 0.1875
- enc_gain: float32 [1024], P(('mesh', 'sub')), may hold values from 0.25 to 1.75
- proc_send_weight: bfloat16 [1024, 1024], P(None, ('mesh', 'sub')), may hold values from -0.1875 to 0.1875
- proc_recv_weight: bfloat16 [1024, 1024], P(None, ('mesh', 'sub')), may hold values from -0.1875 to 0.1875
- proc_bias: float32 [1024], P(('mesh', 'sub')), may hold values from -3 to 3
- proc_out_weight: bfloat16 [1024, 1024], P(None, ('mesh', 'sub')), may hold values from -0.1875 to 0.1875
- proc_gain: float32 [1024], P(('mesh', 'sub')), may hold values from 0.25 to 1.75
- dec_send_weight: bfloat16 [1024, 1024], P(None, ('mesh', 'sub')), may hold values from -0.1875 to 0.1875
- dec_recv_weight: bfloat16 [1024, 1024], P(None, ('mesh', 'sub')), may hold values from -0.1875 to 0.1875
- dec_bias: float32 [1024], P(('mesh', 'sub')), may hold values from -3 to 3
- dec_out_weight: bfloat16 [1024, 1024], P(None, ('mesh', 'sub')), may hold values from -0.1875 to 0.1875
- dec_gain: float32 [1024], P(('mesh', 'sub')), may hold values from 0.25 to 1.75
- enc_src: int32 [24, 16], P('groups'), parts along dimension 0, may hold values from 0 to 31, as said below
- enc_count: int32 [24], P('groups'), parts along dimension 0, may hold values from 1 to 16
- proc_nbr: int32 [24, 6], P('groups'), parts along dimension 0, may hold values from 0 to 11, as said below
- dec_src: int32 [64, 3], P('groups'), parts along dimension 0, may hold values from 0 to 11, as said below
Outputs:
- grid_out: bfloat16 [8192, 1024], P(('groups', 'grid'), ('mesh', 'sub')), parts along dimension 0
- mesh_out: bfloat16 [3072, 1024], P(('groups', 'grid'), ('mesh', 'sub')), parts along dimension 0
The draws below stay inside these ranges and needn't reach their ends.
There are 2 independent parts, one for each index of `groups`. The reference program is written for one: setup_inputs(seed, part) draws one part's arguments, and reference() takes and returns one part's arrays. A program takes and returns all parts, laid end to end along the dimension named above; an argument that names none is the same for every part. Nothing has to cross between parts.
Inputs may be any that keep to these rules, and one draw needn't show every extreme that they name: `enc_src`: entries of row m at positions k >= enc_count[m] are no edges. Take the 3 rows m with one and the same m // 3, and count their entries that name blocks b with one and the same b // 8: that count is never over 12, and in every such group of rows it equals 12 for some b // 8, counting only entries that are edges. `proc_nbr`: for mesh block m with o = m // 3, entries 0 and 1 name blocks b with b // 3 = (o - 1) mod 4, entries 2 and 3 with b // 3 = o, entries 4 and 5 with b // 3 = (o + 1) mod 4. `dec_src`: take the 8 rows g with one and the same g // 8, and count their entries that name blocks b with one and the same b // 3: that count is never over 6, and in every such group of rows it equals 6 for some b // 3.
All inputs are finite; a program needn't handle non-finite values.
Results may differ from the reference program's by a relative error of at most 0.014.
Values may be sent and summed in bfloat16 or wider, within the bound.
A program may use at most 64 MiB of HBM per device.

```python
import jax
import jax.numpy as jnp
from jax import lax

D = 1024
F_IN = 256
BLK = 128
K_ENC = 16
DEC_EDGES = 3
NBRS = 6
GB_DEV = 8
MB_DEV = 3
CAP_E = 12
CAP_D = 6
GRID_BLOCKS = 32
MESH_BLOCKS = 12
GRID_NODES = 4096
MESH_NODES = 1536


def pick_slots(key, owners, capacity, entries, per_owner):

    def per_receiver(sub_key):
        key_noise, key_full, key_roll, key_local = jax.random.split(sub_key, 4)
        slot_total = owners * capacity
        noise_bits = jax.random.randint(key_noise, (slot_total,), 0, 65536)
        slot_ids = jnp.arange(slot_total, dtype=jnp.int32)
        full_owner = jax.random.randint(key_full, (), 0, owners)
        boost_bits = jnp.where(slot_ids // capacity == full_owner, 1 << 28, 0)
        scores = noise_bits * slot_total + slot_ids + boost_bits
        ignored, chosen = lax.top_k(scores, entries)
        roll_by = jax.random.randint(key_roll, (), 0, entries)
        placed = jnp.roll(chosen, roll_by)
        owner_of = placed // capacity
        local_block = jax.random.randint(key_local, (entries,), 0, per_owner)
        return ((owner_of * per_owner + local_block).astype(jnp.int32), roll_by)
    receiver_keys = jax.random.split(key, owners)
    return jax.vmap(per_receiver)(receiver_keys)


def encoder_lists(key):
    owners = MESH_BLOCKS // MB_DEV
    entries = MB_DEV * K_ENC
    sources, roll_by = pick_slots(jax.random.fold_in(key, 17), owners, CAP_E, entries, GB_DEV)
    forced_at = (roll_by[:, None] + jnp.arange(CAP_E, dtype=jnp.int32)[None, :]) % entries
    places = jnp.arange(entries, dtype=jnp.int32)
    forced = jnp.any(forced_at[:, :, None] == places[None, None, :], axis=1)
    needed = jnp.max(jnp.where(forced, places % K_ENC + 1, 0).reshape(owners, MB_DEV, K_ENC), axis=2)
    drawn = jax.random.randint(jax.random.fold_in(key, 23), (owners, MB_DEV), 1, K_ENC + 1)
    row_ids = jnp.arange(MB_DEV, dtype=jnp.int32)[None, :]
    drawn = jnp.where(row_ids == 0, K_ENC, jnp.where(row_ids == MB_DEV - 1, 1, drawn))
    counts = jnp.maximum(drawn, needed).astype(jnp.int32)
    return (sources.reshape(MESH_BLOCKS, K_ENC), counts.reshape(MESH_BLOCKS))


def draw_enc_src(key, part):
    return encoder_lists(key)[0]


def draw_enc_count(key, part):
    return encoder_lists(key)[1]


def draw_dec_src(key, part):
    owners = GRID_BLOCKS // GB_DEV
    sources, roll_by = pick_slots(jax.random.fold_in(key, 31), owners, CAP_D, GB_DEV * DEC_EDGES, MB_DEV)
    return sources.reshape(GRID_BLOCKS, DEC_EDGES)


def draw_proc_nbr(key, part):
    owners = MESH_BLOCKS // MB_DEV
    offsets = jnp.array([-1, -1, 0, 0, 1, 1], dtype=jnp.int32)
    home_owner = jnp.arange(MESH_BLOCKS, dtype=jnp.int32) // MB_DEV
    target = (home_owner[:, None] + offsets[None, :] + owners) % owners
    local_block = jax.random.randint(jax.random.fold_in(key, 41), (MESH_BLOCKS, NBRS), 0, MB_DEV)
    return (target * MB_DEV + local_block).astype(jnp.int32)


def steps_of(key, dims, cuts, low, top_value):
    def one(dim, shards_of):
        heights = jax.random.uniform(jax.random.fold_in(jax.random.fold_in(key, 6), dim), (shards_of,), jnp.float32, low / len(cuts), top_value / len(cuts))
        return jnp.repeat(jnp.exp(heights), dims[dim] // shards_of).reshape((-1,) + (1,) * (len(dims) - dim - 1))

    level = one(*cuts[0])
    for cut in cuts[1:]:
        level = level * one(*cut)
    return level


def bell_draw(own_key, dims, spread, limit, pieces=(), kind=jnp.bfloat16):
    level = steps_of(own_key, dims, pieces, -0.22, 0.18) if pieces else 1.0
    values = jax.random.normal(own_key, dims, jnp.float32) * spread * level
    return jnp.minimum(jnp.maximum(values, -limit), limit).astype(kind)


def setup_inputs(seed: int = 0, part: int = 0) -> dict:
    keys = jax.random.split(jax.random.key(seed), 24)
    part_splits = jax.random.split(jax.random.fold_in(keys[23], part), 24)
    grid_feat = bell_draw(part_splits[0], (GRID_NODES, F_IN), 1.0, 6.0, ((0, 4),))
    mesh_state = bell_draw(part_splits[1], (MESH_NODES, D), 1.0, 6.0, ((0, 4), (1, 4)))
    embed_weight = bell_draw(keys[2], (F_IN, D), F_IN ** -0.5, 0.375, ((1, 4),))
    embed_gain = jnp.clip(1.0 + 0.15 * jax.random.normal(keys[3], (D,), jnp.float32), 0.25, 1.75)
    enc_send_weight = bell_draw(keys[4], (D, D), D ** -0.5, 0.1875, ((1, 4),))
    enc_recv_weight = bell_draw(keys[5], (D, D), D ** -0.5, 0.1875, ((1, 4),))
    enc_bias = bell_draw(keys[6], (D,), 0.5, 3.0, ((0, 4),), jnp.float32)
    enc_out_weight = bell_draw(keys[7], (D, D), D ** -0.5, 0.1875, ((1, 4),))
    enc_gain = jnp.clip(1.0 + 0.15 * jax.random.normal(keys[8], (D,), jnp.float32), 0.25, 1.75)
    proc_send_weight = bell_draw(keys[9], (D, D), D ** -0.5, 0.1875, ((1, 4),))
    proc_recv_weight = bell_draw(keys[10], (D, D), D ** -0.5, 0.1875, ((1, 4),))
    proc_bias = bell_draw(keys[11], (D,), 0.5, 3.0, ((0, 4),), jnp.float32)
    proc_out_weight = bell_draw(keys[12], (D, D), D ** -0.5, 0.1875, ((1, 4),))
    proc_gain = jnp.clip(1.0 + 0.15 * jax.random.normal(keys[13], (D,), jnp.float32), 0.25, 1.75)
    dec_send_weight = bell_draw(keys[14], (D, D), D ** -0.5, 0.1875, ((1, 4),))
    dec_recv_weight = bell_draw(keys[15], (D, D), D ** -0.5, 0.1875, ((1, 4),))
    dec_bias = bell_draw(keys[16], (D,), 0.5, 3.0, ((0, 4),), jnp.float32)
    dec_out_weight = bell_draw(keys[17], (D, D), D ** -0.5, 0.1875, ((1, 4),))
    dec_gain = jnp.clip(1.0 + 0.15 * jax.random.normal(keys[18], (D,), jnp.float32), 0.25, 1.75)
    enc_src = draw_enc_src(jax.random.fold_in(jax.random.fold_in(keys[23], part), 71), part)
    enc_count = draw_enc_count(jax.random.fold_in(jax.random.fold_in(keys[23], part), 71), part)
    proc_nbr = draw_proc_nbr(jax.random.fold_in(jax.random.fold_in(keys[23], part), 71), part)
    dec_src = draw_dec_src(jax.random.fold_in(jax.random.fold_in(keys[23], part), 71), part)
    return {"grid_feat": grid_feat, "mesh_state": mesh_state, "embed_weight": embed_weight, "embed_gain": embed_gain, "enc_send_weight": enc_send_weight, "enc_recv_weight": enc_recv_weight, "enc_bias": enc_bias, "enc_out_weight": enc_out_weight, "enc_gain": enc_gain, "proc_send_weight": proc_send_weight, "proc_recv_weight": proc_recv_weight, "proc_bias": proc_bias, "proc_out_weight": proc_out_weight, "proc_gain": proc_gain, "dec_send_weight": dec_send_weight, "dec_recv_weight": dec_recv_weight, "dec_bias": dec_bias, "dec_out_weight": dec_out_weight, "dec_gain": dec_gain, "enc_src": enc_src, "enc_count": enc_count, "proc_nbr": proc_nbr, "dec_src": dec_src}


def layer_norm(values, gain):
    row_mean = lax.optimization_barrier(jnp.mean(values, axis=-1, keepdims=True))
    centred = values - row_mean
    row_var = lax.optimization_barrier(jnp.mean(centred * centred, axis=-1, keepdims=True))
    return centred * lax.rsqrt(row_var + 1e-05) * gain

def edge_sums(sender, receiver, bias, sources, edge_mask):

    def per_block(block_items):
        source_rows, receiver_block, mask_row = block_items
        picked = jnp.take(sender, source_rows, axis=0).astype(jnp.float32)
        active = jax.nn.silu(picked + receiver_block[None] + bias)
        return lax.optimization_barrier(jnp.sum(active * mask_row[:, None, None], axis=0))
    return lax.map(per_block, (sources, receiver, edge_mask)).astype(jnp.bfloat16)

def reference(grid_feat, mesh_state, embed_weight, embed_gain, enc_send_weight, enc_recv_weight, enc_bias, enc_out_weight, enc_gain, proc_send_weight, proc_recv_weight, proc_bias, proc_out_weight, proc_gain, dec_send_weight, dec_recv_weight, dec_bias, dec_out_weight, dec_gain, enc_src, enc_count, proc_nbr, dec_src):
    grid_pre = jnp.dot(grid_feat, embed_weight, preferred_element_type=jnp.float32)
    grid_state = layer_norm(grid_pre, embed_gain).astype(jnp.bfloat16)
    enc_send = jnp.dot(grid_state, enc_send_weight, preferred_element_type=jnp.float32).astype(jnp.bfloat16).reshape(GRID_BLOCKS, BLK, D)
    enc_recv = jnp.dot(mesh_state, enc_recv_weight, preferred_element_type=jnp.float32).reshape(MESH_BLOCKS, BLK, D)
    enc_mask = (jnp.arange(K_ENC, dtype=jnp.int32)[None, :] < enc_count[:, None]).astype(jnp.float32)
    enc_hidden = edge_sums(enc_send, enc_recv, enc_bias, enc_src, enc_mask).reshape(MESH_NODES, D)
    enc_out = jnp.dot(enc_hidden, enc_out_weight, preferred_element_type=jnp.float32)
    mesh_mid = (mesh_state.astype(jnp.float32) + layer_norm(enc_out, enc_gain)).astype(jnp.bfloat16)
    proc_send = jnp.dot(mesh_mid, proc_send_weight, preferred_element_type=jnp.float32).astype(jnp.bfloat16).reshape(MESH_BLOCKS, BLK, D)
    proc_recv = jnp.dot(mesh_mid, proc_recv_weight, preferred_element_type=jnp.float32).reshape(MESH_BLOCKS, BLK, D)
    proc_mask = jnp.ones((MESH_BLOCKS, NBRS), jnp.float32)
    proc_hidden = edge_sums(proc_send, proc_recv, proc_bias, proc_nbr, proc_mask).reshape(MESH_NODES, D)
    proc_out = jnp.dot(proc_hidden, proc_out_weight, preferred_element_type=jnp.float32)
    mesh_out = (mesh_mid.astype(jnp.float32) + layer_norm(proc_out, proc_gain)).astype(jnp.bfloat16)
    dec_send = jnp.dot(mesh_out, dec_send_weight, preferred_element_type=jnp.float32).astype(jnp.bfloat16).reshape(MESH_BLOCKS, BLK, D)
    dec_recv = jnp.dot(grid_state, dec_recv_weight, preferred_element_type=jnp.float32).reshape(GRID_BLOCKS, BLK, D)
    dec_mask = jnp.ones((GRID_BLOCKS, DEC_EDGES), jnp.float32)
    dec_hidden = edge_sums(dec_send, dec_recv, dec_bias, dec_src, dec_mask).reshape(GRID_NODES, D)
    dec_out = jnp.dot(dec_hidden, dec_out_weight, preferred_element_type=jnp.float32)
    grid_out = (grid_state.astype(jnp.float32) + layer_norm(dec_out, dec_gain)).astype(jnp.bfloat16)
    return (grid_out, mesh_out)
```

```python
import functools

import jax
import jax.numpy as jnp
from jax import lax
from jax.experimental import pallas as pl
from jax.experimental.pallas import tpu as pltpu
from jax.sharding import PartitionSpec as P

BLK = 128
EPSILON = 1e-05
MESH_ID = pl.DeviceIdType.MESH
F32 = jnp.float32
BF16 = jnp.bfloat16
SUBROWS = 32


class Drain:
    def __init__(self):
        self.sent = []

    def send(self, src, dst, send_sem, recv_sem, device):
        copy = pltpu.make_async_remote_copy(
            src_ref=src, dst_ref=dst, send_sem=send_sem, recv_sem=recv_sem,
            device_id=device, device_id_type=MESH_ID,
        )
        copy.start()
        self.sent.append(copy)

    def arrived(self, dst, send_sem, recv_sem, device):
        pltpu.make_async_remote_copy(
            src_ref=dst, dst_ref=dst, send_sem=send_sem, recv_sem=recv_sem,
            device_id=device, device_id_type=MESH_ID,
        ).wait_recv()

    def finish(self):
        for copy in self.sent:
            copy.wait_send()


class Gather:
    def __init__(self, drain, sizes, place, view, sems, chunks):
        self.drain, self.view = drain, view
        self.xs, self.xr, self.ss, self.sr = sems
        self.mx, self.subs = sizes
        self.m, self.s = place
        self.chunks = chunks

    def shard(self, j, t):
        return lax.rem(self.m + self.mx - j, self.mx) * self.subs + lax.rem(
            self.s + self.subs - t, self.subs
        )

    def xi(self, c, j):
        return c * self.mx + j

    def si(self, c, t, j):
        return (c * self.subs + t) * self.mx + j

    def sib(self, t):
        return {"sub": lax.rem(self.s + t, self.subs)}

    def peer(self, j):
        return {"mesh": lax.rem(self.m + j, self.mx)}

    def issue(self, c, src=None):
        mine = self.view(self.shard(0, 0), c)
        src = mine if src is None else src
        for j in range(1, self.mx):
            i = self.xi(c, j)
            self.drain.send(src, mine, self.xs.at[i], self.xr.at[i], self.peer(j))
        for t in range(1, self.subs):
            i = self.si(c, t, 0)
            self.drain.send(src, mine, self.ss.at[i], self.sr.at[i], self.sib(t))

    def forward(self, c):
        for j in range(1, self.mx):
            i = self.xi(c, j)
            ref = self.view(self.shard(j, 0), c)
            self.drain.arrived(ref, self.xs.at[i], self.xr.at[i], self.peer(j))
            for t in range(1, self.subs):
                k = self.si(c, t, j)
                self.drain.send(ref, ref, self.ss.at[k], self.sr.at[k], self.sib(t))

    def finish(self, c):
        for t in range(1, self.subs):
            for j in range(self.mx):
                k = self.si(c, t, j)
                self.drain.arrived(
                    self.view(self.shard(j, t), c), self.ss.at[k], self.sr.at[k], self.sib(t)
                )


def gather_sems(chunks, mx, subs):
    return [pltpu.SemaphoreType.DMA((chunks * mx,))] * 2 + [
        pltpu.SemaphoreType.DMA((chunks * subs * mx,))
    ] * 2


def edges(target, receiver, bias_free, sources):
    @pl.loop(0, BLK // SUBROWS)
    def _(r):
        rows = pl.ds(pl.multiple_of(r * SUBROWS, SUBROWS), SUBROWS)
        base = receiver(rows)
        total = bias_free(rows)
        for load, weight in sources:
            half = load(rows).astype(F32) + base
            active = half + half * jnp.tanh(half)
            if weight is not None:
                active = active * weight
            total = active if total is None else total + active
        target(rows, total)


def kernel(
    sizes, enc_src, enc_count, proc_nbr, dec_src, params, grid_feat, mesh_state, embed_w,
    es_w, er_w, eo_w, ps_w, pr_w, po_w, ds_w, dr_w, do_w,
    grid_out, mesh_out,
    w_es, w_er, w_eo, w_ps, w_pr, w_po, w_ds, w_dr, w_do,
    we_all, par_all, ms_all, feats, wec, m_enc, m_dec, enc_all, enc_recv,
    hid1, out1, mid_all, win, proc_recv, hid2, out2, mo_all, dsend, dec_recv, gstate,
    hid3, dec_out, stats, g_stage,
    lsem,
    we_xs, we_xr, we_ss, we_sr,
    ms_xs, ms_xr, ms_ss, ms_sr,
    h1_xs, h1_xr, h1_ss, h1_sr,
    o1_xs, o1_xr, o1_ss, o1_sr,
    h2_xs, h2_xr, h2_ss, h2_sr,
    o2_xs, o2_xr, o2_ss, o2_sr,
    h3_xs, h3_xr, h3_ss, h3_sr,
    fz_s, fz_r, fx_s, fx_r, fs_s, fs_r,
    pp_s, pp_r, st_s, st_r, wz_s, wz_r, dz_s, dz_r,
):
    owners, mx, subs = sizes
    nf = mx * subs
    o, m, s = lax.axis_index("grid"), lax.axis_index("mesh"), lax.axis_index("sub")
    f_me = m * subs + s
    mc = mesh_state.shape[0]
    cols = mesh_state.shape[2]
    gr, fin = grid_feat.shape
    gc = gr // BLK
    d_all = nf * cols
    part = gr // nf
    drain = Drain()

    loads = []

    def load(src, dst):
        copy = pltpu.make_async_copy(src, dst, lsem.at[len(loads)])
        copy.start()
        loads.append(copy)
        return copy

    l_we = load(embed_w, we_all.at[f_me])
    l_es = load(es_w, w_es)
    l_dr = load(dr_w, w_dr)
    l_feat = load(grid_feat, feats.at[o])
    l_ms = load(mesh_state, ms_all.at[f_me])
    l_er = load(er_w, w_er)
    l_par = load(params, par_all.at[f_me])
    l_eo, l_ps, l_pr, l_po, l_ds, l_do = (
        load(a, b)
        for a, b in ((eo_w, w_eo), (ps_w, w_ps), (pr_w, w_pr), (po_w, w_po), (ds_w, w_ds), (do_w, w_do))
    )

    feature_peers = []
    for j in range(mx):
        for t in range(subs):
            if j or t:
                feature_peers.append(
                    {"mesh": lax.rem(m + j, mx), "sub": lax.rem(s + t, subs)}
                )
    grid_peers = [{"grid": lax.rem(o + j, owners)} for j in range(1, owners)]
    barrier = pltpu.get_barrier_semaphore()
    for device in feature_peers + grid_peers:
        pl.semaphore_signal(barrier, inc=1, device_id=device, device_id_type=MESH_ID)
    pl.semaphore_wait(barrier, len(feature_peers) + len(grid_peers))

    def gather(view, sems, chunks):
        return Gather(drain, (mx, subs), (m, s), view, sems, chunks)

    g_we = gather(lambda f, c: we_all.at[f], (we_xs, we_xr, we_ss, we_sr), 1)
    g_ms = gather(lambda f, c: ms_all.at[f], (ms_xs, ms_xr, ms_ss, ms_sr), 1)
    block_view = lambda buf: (lambda f, c: buf.at[f, c])
    g_h1 = gather(block_view(hid1), (h1_xs, h1_xr, h1_ss, h1_sr), mc)
    g_o1 = gather(block_view(out1), (o1_xs, o1_xr, o1_ss, o1_sr), mc)
    g_h2 = gather(block_view(hid2), (h2_xs, h2_xr, h2_ss, h2_sr), mc)
    g_o2 = gather(block_view(out2), (o2_xs, o2_xr, o2_ss, o2_sr), mc)
    g_h3 = gather(block_view(hid3), (h3_xs, h3_xr, h3_ss, h3_sr), gc)

    def peer_shard(p):
        j, t = (p + 1) // subs, (p + 1) % subs
        return lax.rem(m + mx - j, mx) * subs + lax.rem(s + subs - t, subs)

    g_we.issue(0, embed_w)
    for p, device in enumerate(feature_peers):
        drain.send(params, par_all.at[f_me], pp_s.at[p], pp_r.at[p], device)
    my_rows = pl.ds(pl.multiple_of(f_me * part, part), part)
    near = sorted(range(1, owners), key=lambda j: (min(j, owners - j), j))
    for j in sorted(range(1, owners), key=lambda j: (-min(j, owners - j), j)):
        drain.send(
            grid_feat.at[my_rows], feats.at[o, my_rows], fz_s.at[j], fz_r.at[j], grid_peers[j - 1]
        )
    g_ms.issue(0, mesh_state)

    def feat_view(j, f):
        rows = pl.ds(pl.multiple_of(f * part, part), part)
        return feats.at[lax.rem(o + owners - j, owners), rows]

    feat_gathers = {}
    for j in range(1, owners):
        g = gather(lambda f, c, j=j: feat_view(j, f), (fx_s, fx_r, fs_s, fs_r), owners)
        feat_gathers[j] = g

    g_we.forward(0)
    l_we.wait()
    g_we.finish(0)
    l_par.wait()
    for p, device in enumerate(feature_peers):
        drain.arrived(par_all.at[peer_shard(p)], pp_s.at[p], pp_r.at[p], device)
    l_es.wait()
    l_dr.wait()

    row_sum = None
    for f in range(nf):
        one = jnp.sum(we_all[f].astype(F32), axis=1, keepdims=True)
        row_sum = one if row_sum is None else row_sum + one
    row_mean = row_sum / d_all
    enc_map = dec_map = None
    for f in range(nf):
        centred = we_all[f].astype(F32) - row_mean
        wec[f] = centred.astype(BF16)
        gained = (centred * par_all[f, 0:1, :]).astype(BF16)
        a = jnp.dot(gained, w_es[f * cols : (f + 1) * cols, :], preferred_element_type=F32)
        b = jnp.dot(gained, w_dr[f * cols : (f + 1) * cols, :], preferred_element_type=F32)
        enc_map = a if enc_map is None else enc_map + a
        dec_map = b if dec_map is None else dec_map + b
    m_enc[...] = (0.5 * enc_map).astype(BF16)
    m_dec[...] = (0.5 * dec_map).astype(BF16)

    pair = 2 if gc % 2 == 0 else 1

    def project(owner, own):
        @pl.loop(0, gc // pair)
        def _(i):
            rows = pl.ds(pl.multiple_of(i * (pair * BLK), pair * BLK), pair * BLK)
            x = feats[owner, rows, :]
            squares = None
            for f in range(nf):
                v = jnp.dot(x, wec[f], preferred_element_type=F32)
                one = jnp.sum(v * v, axis=1, keepdims=True)
                squares = one if squares is None else squares + one
            scale = lax.rsqrt(squares / d_all + EPSILON)
            sent = jnp.dot(x, m_enc[...], preferred_element_type=F32) * scale
            blocks = pl.ds(owner * gc + i * pair, pair)
            enc_all[blocks] = sent.reshape(pair, BLK, cols)
            if own:
                got = jnp.dot(x, m_dec[...], preferred_element_type=F32) * scale
                got = got + 0.5 * params[6:7, :]
                dec_recv[pl.ds(i * pair, pair)] = got.reshape(pair, BLK, cols)
                state = jnp.dot(x, wec[f_me], preferred_element_type=F32) * scale
                state = (state * params[0:1, :]).astype(BF16)
                gstate[pl.ds(i * pair, pair)] = state.reshape(pair, BLK, cols)

    l_feat.wait()
    for j in near:
        g = feat_gathers[j]
        drain.arrived(feat_view(j, f_me), fz_s.at[j], fz_r.at[j], grid_peers[j - 1])
        g.issue(j)
    project(o, True)
    for j in near:
        feat_gathers[j].forward(j)
    g_ms.forward(0)
    l_ms.wait()
    g_ms.finish(0)
    l_er.wait()

    def product(buf, b, weight):
        total = None
        for f in range(nf):
            one = jnp.dot(buf[f, b], weight[f * cols : (f + 1) * cols, :], preferred_element_type=F32)
            total = one if total is None else total + one
        return total

    for b in range(mc):
        enc_recv[b] = 0.5 * (product(ms_all, b, w_er) + params[4:5, :])
    for j in near:
        feat_gathers[j].finish(j)
        project(lax.rem(o + owners - j, owners), False)

    fan = enc_src.shape[1]
    for b in range(mc):
        row = o * mc + b
        count = enc_count[row, 0]
        sources = []
        for k in range(fan):
            idx = jnp.clip(enc_src[row, k], 0, owners * gc - 1)
            weight = jnp.where(k < count, 1.0, 0.0).astype(F32)
            sources.append((lambda rows, idx=idx: enc_all[idx, rows, :], weight))

        def put(rows, value, b=b):
            hid1[f_me, b, rows, :] = value.astype(BF16)

        edges(put, lambda rows, b=b: enc_recv[b, rows, :], lambda rows: None, sources)
        g_h1.issue(b)

    def node_layer(g_h, hid, weight, g_o, out):
        for b in range(mc):
            g_h.forward(b)
        for b in range(mc):
            g_h.finish(b)
            out[f_me, b] = product(hid, b, weight).astype(BF16)
            g_o.issue(b)
        for b in range(mc):
            g_o.forward(b)

    def norm_rows(out, old, new, b, gain_row):
        @pl.loop(0, BLK // SUBROWS)
        def _(r):
            rows = pl.ds(pl.multiple_of(r * SUBROWS, SUBROWS), SUBROWS)
            total = None
            for f in range(nf):
                one = jnp.sum(out[f, b, rows, :].astype(F32), axis=1, keepdims=True)
                total = one if total is None else total + one
            mean = total / d_all
            squares = None
            for f in range(nf):
                c = out[f, b, rows, :].astype(F32) - mean
                one = jnp.sum(c * c, axis=1, keepdims=True)
                squares = one if squares is None else squares + one
            scale = lax.rsqrt(squares / d_all + EPSILON)
            for f in range(nf):
                c = out[f, b, rows, :].astype(F32) - mean
                value = c * scale * par_all[f, gain_row : gain_row + 1, :]
                new[f, b, rows, :] = (old[f, b, rows, :].astype(F32) + value).astype(BF16)

    l_eo.wait()
    node_layer(g_h1, hid1, w_eo, g_o1, out1)
    l_ps.wait()
    l_pr.wait()
    left, right = {"grid": lax.rem(o + owners - 1, owners)}, {"grid": lax.rem(o + 1, owners)}
    for b in range(mc):
        g_o1.finish(b)
        norm_rows(out1, ms_all, mid_all, b, 1)
        win[1, b] = (0.5 * product(mid_all, b, w_ps)).astype(BF16)
        drain.send(win.at[1, b], win.at[2, b], wz_s.at[2 * b], wz_r.at[2 * b], left)
        drain.send(win.at[1, b], win.at[0, b], wz_s.at[2 * b + 1], wz_r.at[2 * b + 1], right)
    for b in range(mc):
        proc_recv[b] = 0.5 * (product(mid_all, b, w_pr) + params[5:6, :])
    for b in range(mc):
        drain.arrived(win.at[2, b], wz_s.at[2 * b], wz_r.at[2 * b], left)
        drain.arrived(win.at[0, b], wz_s.at[2 * b + 1], wz_r.at[2 * b + 1], right)
    fan = proc_nbr.shape[1]
    for b in range(mc):
        row = o * mc + b
        sources = []
        for q in range(fan):
            side = q * 3 // fan
            home = lax.rem(o + side - 1 + owners, owners)
            idx = jnp.clip(proc_nbr[row, q] - home * mc, 0, mc - 1)
            sources.append((lambda rows, idx=idx, side=side: win[side, idx, rows, :], None))

        def put(rows, value, b=b):
            hid2[f_me, b, rows, :] = value.astype(BF16)

        edges(put, lambda rows, b=b: proc_recv[b, rows, :], lambda rows: None, sources)
        g_h2.issue(b)
    l_po.wait()
    node_layer(g_h2, hid2, w_po, g_o2, out2)
    l_ds.wait()
    for b in range(mc):
        g_o2.finish(b)
        norm_rows(out2, mid_all, mo_all, b, 2)
        dsend[o * mc + b] = (0.5 * product(mo_all, b, w_ds)).astype(BF16)
        for j in range(1, owners):
            i = b * owners + j
            ref = dsend.at[o * mc + b]
            drain.send(ref, ref, dz_s.at[i], dz_r.at[i], grid_peers[j - 1])
    l_out = load(mo_all.at[f_me], mesh_out)
    for b in range(mc):
        for j in near:
            i = b * owners + j
            ref = dsend.at[lax.rem(o + owners - j, owners) * mc + b]
            drain.arrived(ref, dz_s.at[i], dz_r.at[i], grid_peers[j - 1])

    fan = dec_src.shape[1]
    for g in range(gc):
        sources = []
        for e in range(fan):
            idx = jnp.clip(dec_src[o * gc + g, e], 0, owners * mc - 1)
            sources.append((lambda rows, idx=idx: dsend[idx, rows, :], None))

        def put(rows, value, g=g):
            hid3[f_me, g, rows, :] = value.astype(BF16)

        edges(put, lambda rows, g=g: dec_recv[g, rows, :], lambda rows: None, sources)
        g_h3.issue(g)

    l_do.wait()
    eye = lax.broadcasted_iota(jnp.int32, (BLK, BLK), 0) == lax.broadcasted_iota(
        jnp.int32, (BLK, BLK), 1
    )

    top = lax.broadcasted_iota(jnp.int32, (8, BLK), 0) == 0

    def to_row(column):
        return jnp.sum(jnp.where(eye, column, 0.0), axis=0, keepdims=True)

    def to_column(row):
        return jnp.sum(jnp.where(eye, row, 0.0), axis=1, keepdims=True)

    def decode(g):
        g_h3.finish(g)
        value = product(hid3, g, w_do)
        dec_out[g] = value
        sums = to_row(jnp.sum(value, axis=1, keepdims=True))
        squares = to_row(jnp.sum(value * value, axis=1, keepdims=True))
        stats[f_me, g] = jnp.where(top, sums, squares)
        for p, device in enumerate(feature_peers):
            i = g * nf + p
            drain.send(stats.at[f_me, g], stats.at[f_me, g], st_s.at[i], st_r.at[i], device)

    outs = []

    def complete(g):
        for p, device in enumerate(feature_peers):
            i = g * nf + p
            drain.arrived(stats.at[peer_shard(p), g], st_s.at[i], st_r.at[i], device)
        total, squares = stats[0, g, 0:1, :], stats[0, g, 1:2, :]
        for f in range(1, nf):
            total = total + stats[f, g, 0:1, :]
            squares = squares + stats[f, g, 1:2, :]
        mean = total / d_all
        scale = lax.rsqrt(squares / d_all - mean * mean + EPSILON)
        value = (dec_out[g] - to_column(mean)) * to_column(scale) * params[3:4, :]
        g_stage[g] = (gstate[g].astype(F32) + value).astype(BF16)
        outs.append(load(g_stage.at[g], grid_out.at[g]))

    for g in range(gc):
        g_h3.forward(g)
        if g >= 1:
            decode(g - 1)
        if g >= 3:
            complete(g - 3)
    decode(gc - 1)
    for g in range(max(gc - 3, 0), gc):
        complete(g)
    l_out.wait()
    for copy in outs:
        copy.wait()
    drain.finish()


def on_device(
    grid_feat, mesh_state, embed_weight, embed_gain, enc_send_weight, enc_recv_weight, enc_bias,
    enc_out_weight, enc_gain, proc_send_weight, proc_recv_weight, proc_bias, proc_out_weight,
    proc_gain, dec_send_weight, dec_recv_weight, dec_bias, dec_out_weight, dec_gain,
    enc_src, enc_count, proc_nbr, dec_src,
):
    owners, mx, subs = (lax.axis_size(a) for a in ("grid", "mesh", "sub"))
    nf = mx * subs
    mr, cols = mesh_state.shape
    gr, fin = grid_feat.shape
    mc, gc = mr // BLK, gr // BLK
    depth = enc_send_weight.shape[0]
    params = jnp.stack(
        [embed_gain, enc_gain, proc_gain, dec_gain, enc_bias, proc_bias, dec_bias, dec_bias]
    )
    smem = pl.BlockSpec(memory_space=pltpu.SMEM)
    vmem = pl.BlockSpec(memory_space=pltpu.VMEM)
    hbm = pl.BlockSpec(memory_space=pl.ANY)
    dma = pltpu.SemaphoreType.DMA
    scratch = [pltpu.VMEM((depth, cols), BF16)] * 9
    scratch += [
        pltpu.VMEM((nf, fin, cols), BF16),
        pltpu.VMEM((nf, 8, cols), F32),
        pltpu.VMEM((nf, mc, BLK, cols), BF16),
        pltpu.VMEM((owners, gr, fin), BF16),
        pltpu.VMEM((nf, fin, cols), BF16),
        pltpu.VMEM((fin, cols), BF16),
        pltpu.VMEM((fin, cols), BF16),
        pltpu.VMEM((owners * gc, BLK, cols), F32),
        pltpu.VMEM((mc, BLK, cols), F32),
        pltpu.VMEM((nf, mc, BLK, cols), BF16),
        pltpu.VMEM((nf, mc, BLK, cols), BF16),
        pltpu.VMEM((nf, mc, BLK, cols), BF16),
        pltpu.VMEM((3, mc, BLK, cols), BF16),
        pltpu.VMEM((mc, BLK, cols), F32),
        pltpu.VMEM((nf, mc, BLK, cols), BF16),
        pltpu.VMEM((nf, mc, BLK, cols), BF16),
        pltpu.VMEM((nf, mc, BLK, cols), BF16),
        pltpu.VMEM((owners * mc, BLK, cols), BF16),
        pltpu.VMEM((gc, BLK, cols), F32),
        pltpu.VMEM((gc, BLK, cols), BF16),
        pltpu.VMEM((nf, gc, BLK, cols), BF16),
        pltpu.VMEM((gc, BLK, cols), F32),
        pltpu.VMEM((nf, gc, 8, BLK), F32),
        pltpu.VMEM((gc, BLK, cols), BF16),
    ]
    scratch += [dma((14 + gc,))]
    for chunks in (1, 1, mc, mc, mc, mc, gc):
        scratch += gather_sems(chunks, mx, subs)
    scratch += [dma((owners,))] * 2
    scratch += [dma((owners * mx,))] * 2 + [dma((owners * subs * mx,))] * 2
    scratch += [dma((nf,))] * 2 + [dma((gc * nf,))] * 2
    scratch += [dma((2 * mc,))] * 2 + [dma((mc * owners,))] * 2
    grid_out, mesh_out = pl.pallas_call(
        functools.partial(kernel, (owners, mx, subs)),
        out_shape=(
            jax.ShapeDtypeStruct((gc, BLK, cols), BF16),
            jax.ShapeDtypeStruct((mc, BLK, cols), BF16),
        ),
        in_specs=[smem] * 4 + [vmem] + [hbm] * 12,
        out_specs=(hbm, hbm),
        scratch_shapes=scratch,
        compiler_params=pltpu.CompilerParams(
            collective_id=0, has_side_effects=True, vmem_limit_bytes=62 * 1024 * 1024
        ),
        name="graph_step",
    )(
        enc_src, enc_count.reshape(-1, 1), proc_nbr, dec_src, params, grid_feat,
        mesh_state.reshape(mc, BLK, cols), embed_weight, enc_send_weight, enc_recv_weight,
        enc_out_weight, proc_send_weight, proc_recv_weight, proc_out_weight, dec_send_weight,
        dec_recv_weight, dec_out_weight,
    )
    return grid_out.reshape(gr, cols), mesh_out.reshape(mr, cols)


def solution(mesh):
    rows = P(("groups", "grid"), None)
    both = P(("groups", "grid"), ("mesh", "sub"))
    weight = P(None, ("mesh", "sub"))
    vector = P(("mesh", "sub"))
    return jax.shard_map(
        on_device,
        mesh=mesh,
        in_specs=(
            rows, both, weight, vector, weight, weight, vector, weight, vector, weight, weight,
            vector, weight, vector, weight, weight, vector, weight, vector,
            P("groups", None), P("groups"), P("groups", None), P("groups", None),
        ),
        out_specs=(both, both),
        check_vma=False,
    )
```

```python
import functools

import jax
import jax.numpy as jnp
from jax import lax
from jax.experimental import pallas as pl
from jax.experimental.pallas import tpu as pltpu
from jax.sharding import PartitionSpec as P

BLK = 128
EPSILON = 1e-05
MESH_ID = pl.DeviceIdType.MESH
F32 = jnp.float32
BF16 = jnp.bfloat16
SUBROWS = 32


class Drain:
    def __init__(self):
        self.sent = []

    def send(self, src, dst, send_sem, recv_sem, device):
        copy = pltpu.make_async_remote_copy(
            src_ref=src, dst_ref=dst, send_sem=send_sem, recv_sem=recv_sem,
            device_id=device, device_id_type=MESH_ID,
        )
        copy.start()
        self.sent.append((None, copy))

    def send_if(self, wanted, src, dst, send_sem, recv_sem, device):
        copy = pltpu.make_async_remote_copy(
            src_ref=src, dst_ref=dst, send_sem=send_sem, recv_sem=recv_sem,
            device_id=device, device_id_type=MESH_ID,
        )

        @pl.when(wanted)
        def _():
            copy.start()

        self.sent.append((wanted, copy))

    def arrived(self, dst, send_sem, recv_sem, device):
        pltpu.make_async_remote_copy(
            src_ref=dst, dst_ref=dst, send_sem=send_sem, recv_sem=recv_sem,
            device_id=device, device_id_type=MESH_ID,
        ).wait_recv()

    def finish(self):
        for wanted, copy in self.sent:
            if wanted is None:
                copy.wait_send()
            else:

                @pl.when(wanted)
                def _(copy=copy):
                    copy.wait_send()


class Gather:
    def __init__(self, drain, sizes, place, view, sems, chunks):
        self.drain, self.view = drain, view
        self.xs, self.xr, self.ss, self.sr = sems
        self.mx, self.subs = sizes
        self.m, self.s = place
        self.chunks = chunks

    def shard(self, j, t):
        return lax.rem(self.m + self.mx - j, self.mx) * self.subs + lax.rem(
            self.s + self.subs - t, self.subs
        )

    def xi(self, c, j):
        return c * self.mx + j

    def si(self, c, t, j):
        return (c * self.subs + t) * self.mx + j

    def sib(self, t):
        return {"sub": lax.rem(self.s + t, self.subs)}

    def peer(self, j):
        return {"mesh": lax.rem(self.m + j, self.mx)}

    def issue(self, c, src=None):
        mine = self.view(self.shard(0, 0), c)
        src = mine if src is None else src
        for j in range(1, self.mx):
            i = self.xi(c, j)
            self.drain.send(src, mine, self.xs.at[i], self.xr.at[i], self.peer(j))
        for t in range(1, self.subs):
            i = self.si(c, t, 0)
            self.drain.send(src, mine, self.ss.at[i], self.sr.at[i], self.sib(t))

    def forward(self, c):
        for j in range(1, self.mx):
            i = self.xi(c, j)
            ref = self.view(self.shard(j, 0), c)
            self.drain.arrived(ref, self.xs.at[i], self.xr.at[i], self.peer(j))
            for t in range(1, self.subs):
                k = self.si(c, t, j)
                self.drain.send(ref, ref, self.ss.at[k], self.sr.at[k], self.sib(t))

    def finish(self, c):
        for t in range(1, self.subs):
            for j in range(self.mx):
                k = self.si(c, t, j)
                self.drain.arrived(
                    self.view(self.shard(j, t), c), self.ss.at[k], self.sr.at[k], self.sib(t)
                )


class Line:
    def __init__(self, drain, owners, o, view, sems):
        self.drain, self.owners, self.o, self.view = drain, owners, o, view
        self.ss, self.rs = sems

    def source(self, i):
        tables = [
            sorted((x for x in range(self.owners) if x != r), key=lambda x: (abs(r - x), x))
            for r in range(self.owners)
        ]
        found = jnp.int32(tables[0][i])
        for r in range(1, self.owners):
            found = jnp.where(self.o == r, jnp.int32(tables[r][i]), found)
        return found

    def issue(self, c, src=None):
        mine = self.view(self.o, c)
        src = mine if src is None else src
        arrive = self.rs.at[c * self.owners + self.o]
        base = c * (self.owners + 1)
        last = self.owners - 1
        right = {"grid": jnp.minimum(self.o + 1, last)}
        left = {"grid": jnp.maximum(self.o - 1, 0)}
        self.drain.send_if(self.o < last, src, mine, self.ss.at[base + self.o], arrive, right)
        self.drain.send_if(self.o > 0, src, mine, self.ss.at[base + self.owners], arrive, left)

    def receive(self, source, c):
        ref = self.view(source, c)
        arrive = self.rs.at[c * self.owners + source]
        sent = self.ss.at[c * (self.owners + 1) + source]
        last = self.owners - 1
        onward = jnp.where(source < self.o, self.o + 1, self.o - 1)
        device = {"grid": jnp.clip(onward, 0, last)}
        self.drain.arrived(ref, sent, arrive, device)
        self.drain.send_if((onward >= 0) & (onward <= last), ref, ref, sent, arrive, device)


def gather_sems(chunks, mx, subs):
    return [pltpu.SemaphoreType.DMA((chunks * mx,))] * 2 + [
        pltpu.SemaphoreType.DMA((chunks * subs * mx,))
    ] * 2


def edges(target, receiver, bias_free, sources):
    @pl.loop(0, BLK // SUBROWS)
    def _(r):
        rows = pl.ds(pl.multiple_of(r * SUBROWS, SUBROWS), SUBROWS)
        base = receiver(rows)
        total = bias_free(rows)
        for load, weight in sources:
            half = load(rows).astype(F32) + base
            active = half + half * jnp.tanh(half)
            if weight is not None:
                active = active * weight
            total = active if total is None else total + active
        target(rows, total)


def kernel(
    sizes, enc_src, enc_count, proc_nbr, dec_src, e_gain, c_gain, p_gain, d_gain,
    e_bias, p_bias, d_bias, grid_feat, mesh_state, embed_w,
    es_w, er_w, eo_w, ps_w, pr_w, po_w, ds_w, dr_w, do_w,
    grid_out, mesh_out,
    w_es, w_er, w_eo, w_ps, w_pr, w_po, w_ds, w_dr, w_do,
    we_all, gains, local, ms_all, feats, wec, m_enc, m_dec, enc_all, enc_recv,
    hid1, out1, mid_all, win, proc_recv, hid2, out2, mo_all, dsend, dec_recv, gstate,
    hid3, dec_out, stats, g_stage,
    lsem,
    we_xs, we_xr, we_ss, we_sr,
    ms_xs, ms_xr, ms_ss, ms_sr,
    h1_xs, h1_xr, h1_ss, h1_sr,
    o1_xs, o1_xr, o1_ss, o1_sr,
    h2_xs, h2_xr, h2_ss, h2_sr,
    o2_xs, o2_xr, o2_ss, o2_sr,
    h3_xs, h3_xr, h3_ss, h3_sr,
    fz_s, fz_r, fx_s, fx_r, fs_s, fs_r,
    pp_s, pp_r, st_s, st_r, wz_s, wz_r, dz_s, dz_r,
):
    owners, mx, subs = sizes
    nf = mx * subs
    o, m, s = lax.axis_index("grid"), lax.axis_index("mesh"), lax.axis_index("sub")
    f_me = m * subs + s
    mc = mesh_state.shape[0]
    cols = mesh_state.shape[2]
    gr, fin = grid_feat.shape
    gc = gr // BLK
    d_all = nf * cols
    part = gr // nf
    drain = Drain()

    loads = []

    def load(src, dst):
        copy = pltpu.make_async_copy(src, dst, lsem.at[len(loads)])
        copy.start()
        loads.append(copy)
        return copy

    l_we = load(embed_w, we_all.at[f_me])
    l_es = load(es_w, w_es)
    l_dr = load(dr_w, w_dr)
    l_feat = load(grid_feat, feats.at[o])
    l_ms = load(mesh_state, ms_all.at[f_me])
    l_er = load(er_w, w_er)
    gain_refs = (e_gain, c_gain, p_gain)
    l_small = [load(ref, gains.at[k, f_me]) for k, ref in enumerate(gain_refs)]
    l_small += [load(ref, local.at[k]) for k, ref in enumerate((d_gain, e_bias, p_bias, d_bias))]
    l_eo, l_ps, l_pr, l_po, l_ds, l_do = (
        load(a, b)
        for a, b in ((eo_w, w_eo), (ps_w, w_ps), (pr_w, w_pr), (po_w, w_po), (ds_w, w_ds), (do_w, w_do))
    )

    feature_peers = []
    for j in range(mx):
        for t in range(subs):
            if j or t:
                feature_peers.append(
                    {"mesh": lax.rem(m + j, mx), "sub": lax.rem(s + t, subs)}
                )
    left, right = {"grid": lax.rem(o + owners - 1, owners)}, {"grid": lax.rem(o + 1, owners)}
    grid_peers = [left, right]
    barrier = pltpu.get_barrier_semaphore()
    for device in feature_peers + grid_peers:
        pl.semaphore_signal(barrier, inc=1, device_id=device, device_id_type=MESH_ID)
    pl.semaphore_wait(barrier, len(feature_peers) + len(grid_peers))

    def gather(view, sems, chunks):
        return Gather(drain, (mx, subs), (m, s), view, sems, chunks)

    g_we = gather(lambda f, c: we_all.at[f], (we_xs, we_xr, we_ss, we_sr), 1)
    g_ms = gather(lambda f, c: ms_all.at[f], (ms_xs, ms_xr, ms_ss, ms_sr), 1)
    block_view = lambda buf: (lambda f, c: buf.at[f, c])
    g_h1 = gather(block_view(hid1), (h1_xs, h1_xr, h1_ss, h1_sr), mc)
    g_o1 = gather(block_view(out1), (o1_xs, o1_xr, o1_ss, o1_sr), mc)
    g_h2 = gather(block_view(hid2), (h2_xs, h2_xr, h2_ss, h2_sr), mc)
    g_o2 = gather(block_view(out2), (o2_xs, o2_xr, o2_ss, o2_sr), mc)
    g_h3 = gather(block_view(hid3), (h3_xs, h3_xr, h3_ss, h3_sr), gc)

    def peer_shard(p):
        j, t = (p + 1) // subs, (p + 1) % subs
        return lax.rem(m + mx - j, mx) * subs + lax.rem(s + subs - t, subs)

    g_we.issue(0, embed_w)
    for p, device in enumerate(feature_peers):
        for k, ref in enumerate(gain_refs):
            i = k * nf + p
            drain.send(ref, gains.at[k, f_me], pp_s.at[i], pp_r.at[i], device)

    def part_rows(f):
        return pl.ds(pl.multiple_of(f * part, part), part)

    z_feat = Line(drain, owners, o, lambda c, _: feats.at[c, part_rows(f_me)], (fz_s, fz_r))
    z_feat.issue(0, grid_feat.at[part_rows(f_me)])
    g_ms.issue(0, mesh_state)
    g_feat = gather(lambda f, c: feats.at[c, part_rows(f)], (fx_s, fx_r, fs_s, fs_r), owners)
    others = [z_feat.source(i) for i in range(owners - 1)]

    g_we.forward(0)
    l_we.wait()
    g_we.finish(0)
    for copy in l_small:
        copy.wait()
    for p, device in enumerate(feature_peers):
        for k in range(len(gain_refs)):
            i = k * nf + p
            drain.arrived(gains.at[k, peer_shard(p)], pp_s.at[i], pp_r.at[i], device)
    l_es.wait()
    l_dr.wait()

    row_sum = None
    for f in range(nf):
        one = jnp.sum(we_all[f].astype(F32), axis=1, keepdims=True)
        row_sum = one if row_sum is None else row_sum + one
    row_mean = row_sum / d_all
    enc_map = dec_map = None
    for f in range(nf):
        centred = we_all[f].astype(F32) - row_mean
        wec[f] = centred.astype(BF16)
        gained = (centred * gains[0, f]).astype(BF16)
        a = jnp.dot(gained, w_es[f * cols : (f + 1) * cols, :], preferred_element_type=F32)
        b = jnp.dot(gained, w_dr[f * cols : (f + 1) * cols, :], preferred_element_type=F32)
        enc_map = a if enc_map is None else enc_map + a
        dec_map = b if dec_map is None else dec_map + b
    m_enc[...] = (0.5 * enc_map).astype(BF16)
    m_dec[...] = (0.5 * dec_map).astype(BF16)

    pair = 2 if gc % 2 == 0 else 1

    def project(owner, own):
        @pl.loop(0, gc // pair)
        def _(i):
            rows = pl.ds(pl.multiple_of(i * (pair * BLK), pair * BLK), pair * BLK)
            x = feats[owner, rows, :]
            squares = None
            for f in range(nf):
                v = jnp.dot(x, wec[f], preferred_element_type=F32)
                one = jnp.sum(v * v, axis=1, keepdims=True)
                squares = one if squares is None else squares + one
            scale = lax.rsqrt(squares / d_all + EPSILON)
            sent = jnp.dot(x, m_enc[...], preferred_element_type=F32) * scale
            blocks = pl.ds(owner * gc + i * pair, pair)
            enc_all[blocks] = sent.reshape(pair, BLK, cols)
            if own:
                got = jnp.dot(x, m_dec[...], preferred_element_type=F32) * scale
                got = got + 0.5 * local[3]
                dec_recv[pl.ds(i * pair, pair)] = got.reshape(pair, BLK, cols)
                state = jnp.dot(x, wec[f_me], preferred_element_type=F32) * scale
                state = (state * gains[0, f_me]).astype(BF16)
                gstate[pl.ds(i * pair, pair)] = state.reshape(pair, BLK, cols)

    l_feat.wait()

    def take(source):
        z_feat.receive(source, 0)
        g_feat.issue(source)

    for source in others[:-1]:
        take(source)
    project(o, True)
    take(others[-1])
    g_ms.forward(0)
    for source in others[:-1]:
        g_feat.forward(source)
    l_ms.wait()
    g_ms.finish(0)
    l_er.wait()

    def product(buf, b, weight):
        total = None
        for f in range(nf):
            one = jnp.dot(buf[f, b], weight[f * cols : (f + 1) * cols, :], preferred_element_type=F32)
            total = one if total is None else total + one
        return total

    for b in range(mc):
        enc_recv[b] = 0.5 * (product(ms_all, b, w_er) + local[1])
    for i, source in enumerate(others):
        if i == len(others) - 1:
            g_feat.forward(source)
        g_feat.finish(source)
        project(source, False)

    fan = enc_src.shape[1]
    for b in range(mc):
        row = o * mc + b
        count = enc_count[row]
        sources = []
        for k in range(fan):
            idx = jnp.clip(enc_src[row, k], 0, owners * gc - 1)
            weight = jnp.where(k < count, 1.0, 0.0).astype(F32)
            sources.append((lambda rows, idx=idx: enc_all[idx, rows, :], weight))

        def put(rows, value, b=b):
            hid1[f_me, b, rows, :] = value.astype(BF16)

        edges(put, lambda rows, b=b: enc_recv[b, rows, :], lambda rows: None, sources)
        g_h1.issue(b)

    def node_layer(g_h, hid, weight, g_o, out):
        for b in range(mc):
            g_h.forward(b)
        for b in range(mc):
            g_h.finish(b)
            out[f_me, b] = product(hid, b, weight).astype(BF16)
            g_o.issue(b)
        for b in range(mc):
            g_o.forward(b)

    def norm_rows(out, old, new, b, gain_row):
        @pl.loop(0, BLK // SUBROWS)
        def _(r):
            rows = pl.ds(pl.multiple_of(r * SUBROWS, SUBROWS), SUBROWS)
            total = None
            for f in range(nf):
                one = jnp.sum(out[f, b, rows, :].astype(F32), axis=1, keepdims=True)
                total = one if total is None else total + one
            mean = total / d_all
            squares = None
            for f in range(nf):
                c = out[f, b, rows, :].astype(F32) - mean
                one = jnp.sum(c * c, axis=1, keepdims=True)
                squares = one if squares is None else squares + one
            scale = lax.rsqrt(squares / d_all + EPSILON)
            for f in range(nf):
                c = out[f, b, rows, :].astype(F32) - mean
                value = c * scale * gains[gain_row, f]
                new[f, b, rows, :] = (old[f, b, rows, :].astype(F32) + value).astype(BF16)

    l_eo.wait()
    node_layer(g_h1, hid1, w_eo, g_o1, out1)
    l_ps.wait()
    l_pr.wait()
    for b in range(mc):
        g_o1.finish(b)
        norm_rows(out1, ms_all, mid_all, b, 1)
        win[1, b] = (0.5 * product(mid_all, b, w_ps)).astype(BF16)
        drain.send(win.at[1, b], win.at[2, b], wz_s.at[2 * b], wz_r.at[2 * b], left)
        drain.send(win.at[1, b], win.at[0, b], wz_s.at[2 * b + 1], wz_r.at[2 * b + 1], right)
    for b in range(mc):
        proc_recv[b] = 0.5 * (product(mid_all, b, w_pr) + local[2])
    for b in range(mc):
        drain.arrived(win.at[2, b], wz_s.at[2 * b], wz_r.at[2 * b], left)
        drain.arrived(win.at[0, b], wz_s.at[2 * b + 1], wz_r.at[2 * b + 1], right)
    fan = proc_nbr.shape[0]
    for b in range(mc):
        row = o * mc + b
        sources = []
        for q in range(fan):
            side = q * 3 // fan
            home = lax.rem(o + side - 1 + owners, owners)
            idx = jnp.clip(proc_nbr[q, row] - home * mc, 0, mc - 1)
            sources.append((lambda rows, idx=idx, side=side: win[side, idx, rows, :], None))

        def put(rows, value, b=b):
            hid2[f_me, b, rows, :] = value.astype(BF16)

        edges(put, lambda rows, b=b: proc_recv[b, rows, :], lambda rows: None, sources)
        g_h2.issue(b)
    l_po.wait()
    node_layer(g_h2, hid2, w_po, g_o2, out2)
    l_ds.wait()
    z_dec = Line(drain, owners, o, lambda c, b: dsend.at[c * mc + b], (dz_s, dz_r))
    for b in range(mc):
        g_o2.finish(b)
        norm_rows(out2, mid_all, mo_all, b, 2)
        dsend[o * mc + b] = (0.5 * product(mo_all, b, w_ds)).astype(BF16)
        z_dec.issue(b)
    l_out = load(mo_all.at[f_me], mesh_out)
    for source in others:
        for b in range(mc):
            z_dec.receive(source, b)

    fan = dec_src.shape[0]
    for g in range(gc):
        sources = []
        for e in range(fan):
            idx = jnp.clip(dec_src[e, o * gc + g], 0, owners * mc - 1)
            sources.append((lambda rows, idx=idx: dsend[idx, rows, :], None))

        def put(rows, value, g=g):
            hid3[f_me, g, rows, :] = value.astype(BF16)

        edges(put, lambda rows, g=g: dec_recv[g, rows, :], lambda rows: None, sources)
        g_h3.issue(g)

    l_do.wait()
    eye = lax.broadcasted_iota(jnp.int32, (BLK, BLK), 0) == lax.broadcasted_iota(
        jnp.int32, (BLK, BLK), 1
    )

    top = lax.broadcasted_iota(jnp.int32, (8, BLK), 0) == 0

    def to_row(column):
        return jnp.sum(jnp.where(eye, column, 0.0), axis=0, keepdims=True)

    def to_column(row):
        return jnp.sum(jnp.where(eye, row, 0.0), axis=1, keepdims=True)

    def decode(g):
        g_h3.finish(g)
        value = product(hid3, g, w_do)
        dec_out[g] = value
        sums = to_row(jnp.sum(value, axis=1, keepdims=True))
        squares = to_row(jnp.sum(value * value, axis=1, keepdims=True))
        stats[f_me, g] = jnp.where(top, sums, squares)
        for p, device in enumerate(feature_peers):
            i = g * nf + p
            drain.send(stats.at[f_me, g], stats.at[f_me, g], st_s.at[i], st_r.at[i], device)

    outs = []

    def complete(g):
        for p, device in enumerate(feature_peers):
            i = g * nf + p
            drain.arrived(stats.at[peer_shard(p), g], st_s.at[i], st_r.at[i], device)
        total, squares = stats[0, g, 0:1, :], stats[0, g, 1:2, :]
        for f in range(1, nf):
            total = total + stats[f, g, 0:1, :]
            squares = squares + stats[f, g, 1:2, :]
        mean = total / d_all
        scale = lax.rsqrt(squares / d_all - mean * mean + EPSILON)
        value = (dec_out[g] - to_column(mean)) * to_column(scale) * local[0]
        g_stage[g] = (gstate[g].astype(F32) + value).astype(BF16)
        outs.append(load(g_stage.at[g], grid_out.at[g]))

    for g in range(gc):
        g_h3.forward(g)
        if g >= 1:
            decode(g - 1)
        if g >= 3:
            complete(g - 3)
    decode(gc - 1)
    for g in range(max(gc - 3, 0), gc):
        complete(g)
    l_out.wait()
    for copy in outs:
        copy.wait()
    drain.finish()


def on_device(
    grid_feat, mesh_state, embed_weight, embed_gain, enc_send_weight, enc_recv_weight, enc_bias,
    enc_out_weight, enc_gain, proc_send_weight, proc_recv_weight, proc_bias, proc_out_weight,
    proc_gain, dec_send_weight, dec_recv_weight, dec_bias, dec_out_weight, dec_gain,
    enc_src, enc_count, proc_nbr, dec_src,
):
    owners, mx, subs = (lax.axis_size(a) for a in ("grid", "mesh", "sub"))
    nf = mx * subs
    mr, cols = mesh_state.shape
    gr, fin = grid_feat.shape
    mc, gc = mr // BLK, gr // BLK
    depth = enc_send_weight.shape[0]
    vectors = (embed_gain, enc_gain, proc_gain, dec_gain, enc_bias, proc_bias, dec_bias)
    smem = pl.BlockSpec(memory_space=pltpu.SMEM)
    hbm = pl.BlockSpec(memory_space=pl.ANY)
    dma = pltpu.SemaphoreType.DMA
    scratch = [pltpu.VMEM((depth, cols), BF16)] * 9
    scratch += [
        pltpu.VMEM((nf, fin, cols), BF16),
        pltpu.VMEM((3, nf, 1, cols), F32),
        pltpu.VMEM((4, 1, cols), F32),
        pltpu.VMEM((nf, mc, BLK, cols), BF16),
        pltpu.VMEM((owners, gr, fin), BF16),
        pltpu.VMEM((nf, fin, cols), BF16),
        pltpu.VMEM((fin, cols), BF16),
        pltpu.VMEM((fin, cols), BF16),
        pltpu.VMEM((owners * gc, BLK, cols), F32),
        pltpu.VMEM((mc, BLK, cols), F32),
        pltpu.VMEM((nf, mc, BLK, cols), BF16),
        pltpu.VMEM((nf, mc, BLK, cols), BF16),
        pltpu.VMEM((nf, mc, BLK, cols), BF16),
        pltpu.VMEM((3, mc, BLK, cols), BF16),
        pltpu.VMEM((mc, BLK, cols), F32),
        pltpu.VMEM((nf, mc, BLK, cols), BF16),
        pltpu.VMEM((nf, mc, BLK, cols), BF16),
        pltpu.VMEM((nf, mc, BLK, cols), BF16),
        pltpu.VMEM((owners * mc, BLK, cols), BF16),
        pltpu.VMEM((gc, BLK, cols), F32),
        pltpu.VMEM((gc, BLK, cols), BF16),
        pltpu.VMEM((nf, gc, BLK, cols), BF16),
        pltpu.VMEM((gc, BLK, cols), F32),
        pltpu.VMEM((nf, gc, 8, BLK), F32),
        pltpu.VMEM((gc, BLK, cols), BF16),
    ]
    scratch += [dma((20 + gc,))]
    for chunks in (1, 1, mc, mc, mc, mc, gc):
        scratch += gather_sems(chunks, mx, subs)
    scratch += [dma((owners + 1,)), dma((owners,))]
    scratch += [dma((owners * mx,))] * 2 + [dma((owners * subs * mx,))] * 2
    scratch += [dma((3 * nf,))] * 2 + [dma((gc * nf,))] * 2
    scratch += [dma((2 * mc,))] * 2 + [dma((mc * (owners + 1),)), dma((mc * owners,))]
    grid_out, mesh_out = pl.pallas_call(
        functools.partial(kernel, (owners, mx, subs)),
        out_shape=(
            jax.ShapeDtypeStruct((gc, BLK, cols), BF16),
            jax.ShapeDtypeStruct((mc, BLK, cols), BF16),
        ),
        in_specs=[smem] * 4 + [hbm] * 19,
        out_specs=(hbm, hbm),
        scratch_shapes=scratch,
        compiler_params=pltpu.CompilerParams(
            collective_id=0, has_side_effects=True, vmem_limit_bytes=62 * 1024 * 1024
        ),
        name="graph_step",
    )(
        enc_src, enc_count, proc_nbr.T, dec_src.T, *(v.reshape(1, cols) for v in vectors), grid_feat,
        mesh_state.reshape(mc, BLK, cols), embed_weight, enc_send_weight, enc_recv_weight,
        enc_out_weight, proc_send_weight, proc_recv_weight, proc_out_weight, dec_send_weight,
        dec_recv_weight, dec_out_weight,
    )
    return grid_out.reshape(gr, cols), mesh_out.reshape(mr, cols)


def solution(mesh):
    rows = P(("groups", "grid"), None)
    both = P(("groups", "grid"), ("mesh", "sub"))
    weight = P(None, ("mesh", "sub"))
    vector = P(("mesh", "sub"))
    return jax.shard_map(
        on_device,
        mesh=mesh,
        in_specs=(
            rows, both, weight, vector, weight, weight, vector, weight, vector, weight, weight,
            vector, weight, vector, weight, weight, vector, weight, vector,
            P("groups", None), P("groups"), P("groups", None), P("groups", None),
        ),
        out_specs=(both, both),
        check_vma=False,
    )
```

```python
import functools

import jax
import jax.numpy as jnp
from jax import lax
from jax.experimental import pallas as pl
from jax.experimental.pallas import tpu as pltpu
from jax.sharding import PartitionSpec as P

BLK = 128
EPSILON = 1e-05
MESH_ID = pl.DeviceIdType.MESH
F32 = jnp.float32
BF16 = jnp.bfloat16
SUBROWS = 32


class Drain:
    def __init__(self):
        self.sent = []

    def send(self, src, dst, send_sem, recv_sem, device):
        copy = pltpu.make_async_remote_copy(
            src_ref=src, dst_ref=dst, send_sem=send_sem, recv_sem=recv_sem,
            device_id=device, device_id_type=MESH_ID,
        )
        copy.start()
        self.sent.append((None, copy))

    def send_if(self, wanted, src, dst, send_sem, recv_sem, device):
        copy = pltpu.make_async_remote_copy(
            src_ref=src, dst_ref=dst, send_sem=send_sem, recv_sem=recv_sem,
            device_id=device, device_id_type=MESH_ID,
        )

        @pl.when(wanted)
        def _():
            copy.start()

        self.sent.append((wanted, copy))

    def arrived(self, dst, send_sem, recv_sem, device):
        pltpu.make_async_remote_copy(
            src_ref=dst, dst_ref=dst, send_sem=send_sem, recv_sem=recv_sem,
            device_id=device, device_id_type=MESH_ID,
        ).wait_recv()

    def finish(self):
        for wanted, copy in self.sent:
            if wanted is None:
                copy.wait_send()
            else:

                @pl.when(wanted)
                def _(copy=copy):
                    copy.wait_send()


class Gather:
    def __init__(self, drain, sizes, place, view, sems, chunks):
        self.drain, self.view = drain, view
        self.xs, self.xr, self.ss, self.sr = sems
        self.mx, self.subs = sizes
        self.m, self.s = place
        self.chunks = chunks

    def shard(self, j, t):
        return lax.rem(self.m + self.mx - j, self.mx) * self.subs + lax.rem(
            self.s + self.subs - t, self.subs
        )

    def xi(self, c, j):
        return c * self.mx + j

    def si(self, c, t, j):
        return (c * self.subs + t) * self.mx + j

    def sib(self, t):
        return {"sub": lax.rem(self.s + t, self.subs)}

    def peer(self, j):
        return {"mesh": lax.rem(self.m + j, self.mx)}

    def issue(self, c, src=None):
        mine = self.view(self.shard(0, 0), c)
        src = mine if src is None else src
        for j in range(1, self.mx):
            i = self.xi(c, j)
            self.drain.send(src, mine, self.xs.at[i], self.xr.at[i], self.peer(j))
        for t in range(1, self.subs):
            i = self.si(c, t, 0)
            self.drain.send(src, mine, self.ss.at[i], self.sr.at[i], self.sib(t))

    def forward(self, c):
        for j in range(1, self.mx):
            i = self.xi(c, j)
            ref = self.view(self.shard(j, 0), c)
            self.drain.arrived(ref, self.xs.at[i], self.xr.at[i], self.peer(j))
            for t in range(1, self.subs):
                k = self.si(c, t, j)
                self.drain.send(ref, ref, self.ss.at[k], self.sr.at[k], self.sib(t))

    def finish(self, c):
        for t in range(1, self.subs):
            for j in range(self.mx):
                k = self.si(c, t, j)
                self.drain.arrived(
                    self.view(self.shard(j, t), c), self.ss.at[k], self.sr.at[k], self.sib(t)
                )


class Line:
    def __init__(self, drain, owners, o, view, sems):
        self.drain, self.owners, self.o, self.view = drain, owners, o, view
        self.ss, self.rs = sems

    def source(self, i):
        tables = [
            sorted((x for x in range(self.owners) if x != r), key=lambda x: (abs(r - x), x))
            for r in range(self.owners)
        ]
        found = jnp.int32(tables[0][i])
        for r in range(1, self.owners):
            found = jnp.where(self.o == r, jnp.int32(tables[r][i]), found)
        return found

    def issue(self, c, src=None):
        mine = self.view(self.o, c)
        src = mine if src is None else src
        arrive = self.rs.at[c * self.owners + self.o]
        base = c * (self.owners + 1)
        last = self.owners - 1
        right = {"grid": jnp.minimum(self.o + 1, last)}
        left = {"grid": jnp.maximum(self.o - 1, 0)}
        self.drain.send_if(self.o < last, src, mine, self.ss.at[base + self.o], arrive, right)
        self.drain.send_if(self.o > 0, src, mine, self.ss.at[base + self.owners], arrive, left)

    def receive(self, source, c):
        ref = self.view(source, c)
        arrive = self.rs.at[c * self.owners + source]
        sent = self.ss.at[c * (self.owners + 1) + source]
        last = self.owners - 1
        onward = jnp.where(source < self.o, self.o + 1, self.o - 1)
        device = {"grid": jnp.clip(onward, 0, last)}
        self.drain.arrived(ref, sent, arrive, device)
        self.drain.send_if((onward >= 0) & (onward <= last), ref, ref, sent, arrive, device)


def gather_sems(chunks, mx, subs):
    return [pltpu.SemaphoreType.DMA((chunks * mx,))] * 2 + [
        pltpu.SemaphoreType.DMA((chunks * subs * mx,))
    ] * 2


def edges(target, receiver, bias_free, sources):
    @pl.loop(0, BLK // SUBROWS)
    def _(r):
        rows = pl.ds(pl.multiple_of(r * SUBROWS, SUBROWS), SUBROWS)
        base = receiver(rows)
        total = bias_free(rows)
        for load, weight in sources:
            half = load(rows).astype(F32) + base
            active = half + half * jnp.tanh(half)
            if weight is not None:
                active = active * weight
            total = active if total is None else total + active
        target(rows, total)


def kernel(
    sizes, enc_src, enc_count, proc_nbr, dec_src, e_gain, c_gain, p_gain, d_gain,
    e_bias, p_bias, d_bias, grid_feat, mesh_state, embed_w,
    es_w, er_w, eo_w, ps_w, pr_w, po_w, ds_w, dr_w, do_w,
    grid_out, mesh_out,
    w_es, w_er, w_eo, w_ps, w_pr, w_po, w_ds, w_dr, w_do,
    we_all, gains, local, ms_all, feats, wec, m_enc, m_dec, enc_all, enc_recv,
    hid1, out1, mid_all, win, proc_recv, hid2, out2, mo_all, dsend, dec_recv, gstate,
    hid3, dec_out, stats, g_stage,
    lsem,
    we_xs, we_xr, we_ss, we_sr,
    ms_xs, ms_xr, ms_ss, ms_sr,
    h1_xs, h1_xr, h1_ss, h1_sr,
    o1_xs, o1_xr, o1_ss, o1_sr,
    h2_xs, h2_xr, h2_ss, h2_sr,
    o2_xs, o2_xr, o2_ss, o2_sr,
    h3_xs, h3_xr, h3_ss, h3_sr,
    fz_s, fz_r, fx_s, fx_r, fs_s, fs_r,
    pp_s, pp_r, st_s, st_r, wz_s, wz_r, dz_s, dz_r,
):
    owners, mx, subs = sizes
    nf = mx * subs
    o, m, s = lax.axis_index("grid"), lax.axis_index("mesh"), lax.axis_index("sub")
    f_me = m * subs + s
    mc = mesh_state.shape[0]
    cols = mesh_state.shape[2]
    gr, fin = grid_feat.shape
    gc = gr // BLK
    d_all = nf * cols
    part = gr // nf
    drain = Drain()

    loads = []

    def load(src, dst):
        copy = pltpu.make_async_copy(src, dst, lsem.at[len(loads)])
        copy.start()
        loads.append(copy)
        return copy

    l_we = load(embed_w, we_all.at[f_me])
    gain_refs = (e_gain, c_gain, p_gain)
    l_small = [load(ref, gains.at[k, f_me]) for k, ref in enumerate(gain_refs)]
    l_small += [load(ref, local.at[k]) for k, ref in enumerate((d_gain, e_bias, p_bias, d_bias))]
    feature_peers = []
    for j in range(mx):
        for t in range(subs):
            if j or t:
                feature_peers.append(
                    {"mesh": lax.rem(m + j, mx), "sub": lax.rem(s + t, subs)}
                )
    left, right = {"grid": lax.rem(o + owners - 1, owners)}, {"grid": lax.rem(o + 1, owners)}
    grid_peers = [left, right]
    barrier = pltpu.get_barrier_semaphore()
    for device in feature_peers + grid_peers:
        pl.semaphore_signal(barrier, inc=1, device_id=device, device_id_type=MESH_ID)
    pl.semaphore_wait(barrier, len(feature_peers) + len(grid_peers))

    def gather(view, sems, chunks):
        return Gather(drain, (mx, subs), (m, s), view, sems, chunks)

    g_we = gather(lambda f, c: we_all.at[f], (we_xs, we_xr, we_ss, we_sr), 1)
    g_ms = gather(lambda f, c: ms_all.at[f], (ms_xs, ms_xr, ms_ss, ms_sr), 1)
    block_view = lambda buf: (lambda f, c: buf.at[f, c])
    g_h1 = gather(block_view(hid1), (h1_xs, h1_xr, h1_ss, h1_sr), mc)
    g_o1 = gather(block_view(out1), (o1_xs, o1_xr, o1_ss, o1_sr), mc)
    g_h2 = gather(block_view(hid2), (h2_xs, h2_xr, h2_ss, h2_sr), mc)
    g_o2 = gather(block_view(out2), (o2_xs, o2_xr, o2_ss, o2_sr), mc)
    g_h3 = gather(block_view(hid3), (h3_xs, h3_xr, h3_ss, h3_sr), gc)

    def peer_shard(p):
        j, t = (p + 1) // subs, (p + 1) % subs
        return lax.rem(m + mx - j, mx) * subs + lax.rem(s + subs - t, subs)

    g_we.issue(0, embed_w)
    for p, device in enumerate(feature_peers):
        for k, ref in enumerate(gain_refs):
            i = k * nf + p
            drain.send(ref, gains.at[k, f_me], pp_s.at[i], pp_r.at[i], device)

    def part_rows(f):
        return pl.ds(pl.multiple_of(f * part, part), part)

    z_feat = Line(drain, owners, o, lambda c, _: feats.at[c, part_rows(f_me)], (fz_s, fz_r))
    z_feat.issue(0, grid_feat.at[part_rows(f_me)])
    g_ms.issue(0, mesh_state)
    l_es = load(es_w, w_es)
    l_dr = load(dr_w, w_dr)
    l_feat = load(grid_feat, feats.at[o])
    l_ms = load(mesh_state, ms_all.at[f_me])
    l_er, l_eo, l_ps, l_pr, l_po, l_ds, l_do = (
        load(a, b)
        for a, b in (
            (er_w, w_er), (eo_w, w_eo), (ps_w, w_ps), (pr_w, w_pr), (po_w, w_po), (ds_w, w_ds),
            (do_w, w_do),
        )
    )
    g_feat = gather(lambda f, c: feats.at[c, part_rows(f)], (fx_s, fx_r, fs_s, fs_r), owners)
    others = [z_feat.source(i) for i in range(owners - 1)]

    g_we.forward(0)
    l_we.wait()
    g_we.finish(0)
    for copy in l_small:
        copy.wait()
    for p, device in enumerate(feature_peers):
        for k in range(len(gain_refs)):
            i = k * nf + p
            drain.arrived(gains.at[k, peer_shard(p)], pp_s.at[i], pp_r.at[i], device)
    l_es.wait()
    l_dr.wait()

    row_sum = None
    for f in range(nf):
        one = jnp.sum(we_all[f].astype(F32), axis=1, keepdims=True)
        row_sum = one if row_sum is None else row_sum + one
    row_mean = row_sum / d_all
    enc_map = dec_map = None
    for f in range(nf):
        centred = we_all[f].astype(F32) - row_mean
        wec[f] = centred.astype(BF16)
        gained = (centred * gains[0, f]).astype(BF16)
        a = jnp.dot(gained, w_es[f * cols : (f + 1) * cols, :], preferred_element_type=F32)
        b = jnp.dot(gained, w_dr[f * cols : (f + 1) * cols, :], preferred_element_type=F32)
        enc_map = a if enc_map is None else enc_map + a
        dec_map = b if dec_map is None else dec_map + b
    m_enc[...] = (0.5 * enc_map).astype(BF16)
    m_dec[...] = (0.5 * dec_map).astype(BF16)

    pair = 2 if gc % 2 == 0 else 1

    def project(owner, own):
        @pl.loop(0, gc // pair)
        def _(i):
            rows = pl.ds(pl.multiple_of(i * (pair * BLK), pair * BLK), pair * BLK)
            x = feats[owner, rows, :]
            squares = None
            for f in range(nf):
                v = jnp.dot(x, wec[f], preferred_element_type=F32)
                one = jnp.sum(v * v, axis=1, keepdims=True)
                squares = one if squares is None else squares + one
            scale = lax.rsqrt(squares / d_all + EPSILON)
            sent = jnp.dot(x, m_enc[...], preferred_element_type=F32) * scale
            blocks = pl.ds(owner * gc + i * pair, pair)
            enc_all[blocks] = sent.reshape(pair, BLK, cols)
            if own:
                got = jnp.dot(x, m_dec[...], preferred_element_type=F32) * scale
                got = got + 0.5 * local[3]
                dec_recv[pl.ds(i * pair, pair)] = got.reshape(pair, BLK, cols)
                state = jnp.dot(x, wec[f_me], preferred_element_type=F32) * scale
                state = (state * gains[0, f_me]).astype(BF16)
                gstate[pl.ds(i * pair, pair)] = state.reshape(pair, BLK, cols)

    l_feat.wait()

    def take(source):
        z_feat.receive(source, 0)
        g_feat.issue(source)

    for source in others[:-1]:
        take(source)
    project(o, True)
    take(others[-1])
    g_ms.forward(0)
    for source in others[:-1]:
        g_feat.forward(source)
    l_ms.wait()
    g_ms.finish(0)
    l_er.wait()

    def product(buf, b, weight):
        total = None
        for f in range(nf):
            one = jnp.dot(buf[f, b], weight[f * cols : (f + 1) * cols, :], preferred_element_type=F32)
            total = one if total is None else total + one
        return total

    for b in range(mc):
        enc_recv[b] = 0.5 * (product(ms_all, b, w_er) + local[1])
    for i, source in enumerate(others):
        if i == len(others) - 1:
            g_feat.forward(source)
        g_feat.finish(source)
        project(source, False)

    fan = enc_src.shape[1]
    for b in range(mc):
        row = o * mc + b
        count = enc_count[row]
        sources = []
        for k in range(fan):
            idx = jnp.clip(enc_src[row, k], 0, owners * gc - 1)
            weight = jnp.where(k < count, 1.0, 0.0).astype(F32)
            sources.append((lambda rows, idx=idx: enc_all[idx, rows, :], weight))

        def put(rows, value, b=b):
            hid1[f_me, b, rows, :] = value.astype(BF16)

        edges(put, lambda rows, b=b: enc_recv[b, rows, :], lambda rows: None, sources)
        g_h1.issue(b)

    def node_layer(g_h, hid, weight, g_o, out):
        g_h.forward(0)
        for b in range(mc):
            if b + 1 < mc:
                g_h.forward(b + 1)
            g_h.finish(b)
            out[f_me, b] = product(hid, b, weight).astype(BF16)
            g_o.issue(b)
        g_o.forward(0)

    def norm_rows(out, old, new, b, gain_row):
        @pl.loop(0, BLK // SUBROWS)
        def _(r):
            rows = pl.ds(pl.multiple_of(r * SUBROWS, SUBROWS), SUBROWS)
            total = None
            for f in range(nf):
                one = jnp.sum(out[f, b, rows, :].astype(F32), axis=1, keepdims=True)
                total = one if total is None else total + one
            mean = total / d_all
            squares = None
            for f in range(nf):
                c = out[f, b, rows, :].astype(F32) - mean
                one = jnp.sum(c * c, axis=1, keepdims=True)
                squares = one if squares is None else squares + one
            scale = lax.rsqrt(squares / d_all + EPSILON)
            for f in range(nf):
                c = out[f, b, rows, :].astype(F32) - mean
                value = c * scale * gains[gain_row, f]
                new[f, b, rows, :] = (old[f, b, rows, :].astype(F32) + value).astype(BF16)

    l_eo.wait()
    node_layer(g_h1, hid1, w_eo, g_o1, out1)
    l_ps.wait()
    l_pr.wait()
    for b in range(mc):
        if b + 1 < mc:
            g_o1.forward(b + 1)
        g_o1.finish(b)
        norm_rows(out1, ms_all, mid_all, b, 1)
        win[1, b] = (0.5 * product(mid_all, b, w_ps)).astype(BF16)
        drain.send(win.at[1, b], win.at[2, b], wz_s.at[2 * b], wz_r.at[2 * b], left)
        drain.send(win.at[1, b], win.at[0, b], wz_s.at[2 * b + 1], wz_r.at[2 * b + 1], right)
    for b in range(mc):
        proc_recv[b] = 0.5 * (product(mid_all, b, w_pr) + local[2])
    for b in range(mc):
        drain.arrived(win.at[2, b], wz_s.at[2 * b], wz_r.at[2 * b], left)
        drain.arrived(win.at[0, b], wz_s.at[2 * b + 1], wz_r.at[2 * b + 1], right)
    fan = proc_nbr.shape[0]
    for b in range(mc):
        row = o * mc + b
        sources = []
        for q in range(fan):
            side = q * 3 // fan
            home = lax.rem(o + side - 1 + owners, owners)
            idx = jnp.clip(proc_nbr[q, row] - home * mc, 0, mc - 1)
            sources.append((lambda rows, idx=idx, side=side: win[side, idx, rows, :], None))

        def put(rows, value, b=b):
            hid2[f_me, b, rows, :] = value.astype(BF16)

        edges(put, lambda rows, b=b: proc_recv[b, rows, :], lambda rows: None, sources)
        g_h2.issue(b)
    l_po.wait()
    node_layer(g_h2, hid2, w_po, g_o2, out2)
    l_ds.wait()
    z_dec = Line(drain, owners, o, lambda c, b: dsend.at[c * mc + b], (dz_s, dz_r))
    for b in range(mc):
        if b + 1 < mc:
            g_o2.forward(b + 1)
        g_o2.finish(b)
        norm_rows(out2, mid_all, mo_all, b, 2)
        dsend[o * mc + b] = (0.5 * product(mo_all, b, w_ds)).astype(BF16)
        z_dec.issue(b)
    l_out = load(mo_all.at[f_me], mesh_out)
    for source in others:
        for b in range(mc):
            z_dec.receive(source, b)

    fan = dec_src.shape[0]
    for g in range(gc):
        sources = []
        for e in range(fan):
            idx = jnp.clip(dec_src[e, o * gc + g], 0, owners * mc - 1)
            sources.append((lambda rows, idx=idx: dsend[idx, rows, :], None))

        def put(rows, value, g=g):
            hid3[f_me, g, rows, :] = value.astype(BF16)

        edges(put, lambda rows, g=g: dec_recv[g, rows, :], lambda rows: None, sources)
        g_h3.issue(g)

    l_do.wait()
    eye = lax.broadcasted_iota(jnp.int32, (BLK, BLK), 0) == lax.broadcasted_iota(
        jnp.int32, (BLK, BLK), 1
    )

    top = lax.broadcasted_iota(jnp.int32, (8, BLK), 0) == 0

    def to_row(column):
        return jnp.sum(jnp.where(eye, column, 0.0), axis=0, keepdims=True)

    def to_column(row):
        return jnp.sum(jnp.where(eye, row, 0.0), axis=1, keepdims=True)

    def decode(g):
        g_h3.finish(g)
        value = product(hid3, g, w_do)
        dec_out[g] = value
        sums = to_row(jnp.sum(value, axis=1, keepdims=True))
        squares = to_row(jnp.sum(value * value, axis=1, keepdims=True))
        stats[f_me, g] = jnp.where(top, sums, squares)
        for p, device in enumerate(feature_peers):
            i = g * nf + p
            drain.send(stats.at[f_me, g], stats.at[f_me, g], st_s.at[i], st_r.at[i], device)

    outs = []

    def complete(g):
        for p, device in enumerate(feature_peers):
            i = g * nf + p
            drain.arrived(stats.at[peer_shard(p), g], st_s.at[i], st_r.at[i], device)
        total, squares = stats[0, g, 0:1, :], stats[0, g, 1:2, :]
        for f in range(1, nf):
            total = total + stats[f, g, 0:1, :]
            squares = squares + stats[f, g, 1:2, :]
        mean = total / d_all
        scale = lax.rsqrt(squares / d_all - mean * mean + EPSILON)
        value = (dec_out[g] - to_column(mean)) * to_column(scale) * local[0]
        g_stage[g] = (gstate[g].astype(F32) + value).astype(BF16)
        outs.append(load(g_stage.at[g], grid_out.at[g]))

    for g in range(gc):
        g_h3.forward(g)
        if g >= 1:
            decode(g - 1)
        if g >= 3:
            complete(g - 3)
    decode(gc - 1)
    for g in range(max(gc - 3, 0), gc):
        complete(g)
    l_out.wait()
    for copy in outs:
        copy.wait()
    drain.finish()


def on_device(
    grid_feat, mesh_state, embed_weight, embed_gain, enc_send_weight, enc_recv_weight, enc_bias,
    enc_out_weight, enc_gain, proc_send_weight, proc_recv_weight, proc_bias, proc_out_weight,
    proc_gain, dec_send_weight, dec_recv_weight, dec_bias, dec_out_weight, dec_gain,
    enc_src, enc_count, proc_nbr, dec_src,
):
    owners, mx, subs = (lax.axis_size(a) for a in ("grid", "mesh", "sub"))
    nf = mx * subs
    mr, cols = mesh_state.shape
    gr, fin = grid_feat.shape
    mc, gc = mr // BLK, gr // BLK
    depth = enc_send_weight.shape[0]
    vectors = (embed_gain, enc_gain, proc_gain, dec_gain, enc_bias, proc_bias, dec_bias)
    smem = pl.BlockSpec(memory_space=pltpu.SMEM)
    hbm = pl.BlockSpec(memory_space=pl.ANY)
    dma = pltpu.SemaphoreType.DMA
    scratch = [pltpu.VMEM((depth, cols), BF16)] * 9
    scratch += [
        pltpu.VMEM((nf, fin, cols), BF16),
        pltpu.VMEM((3, nf, 1, cols), F32),
        pltpu.VMEM((4, 1, cols), F32),
        pltpu.VMEM((nf, mc, BLK, cols), BF16),
        pltpu.VMEM((owners, gr, fin), BF16),
        pltpu.VMEM((nf, fin, cols), BF16),
        pltpu.VMEM((fin, cols), BF16),
        pltpu.VMEM((fin, cols), BF16),
        pltpu.VMEM((owners * gc, BLK, cols), F32),
        pltpu.VMEM((mc, BLK, cols), F32),
        pltpu.VMEM((nf, mc, BLK, cols), BF16),
        pltpu.VMEM((nf, mc, BLK, cols), BF16),
        pltpu.VMEM((nf, mc, BLK, cols), BF16),
        pltpu.VMEM((3, mc, BLK, cols), BF16),
        pltpu.VMEM((mc, BLK, cols), F32),
        pltpu.VMEM((nf, mc, BLK, cols), BF16),
        pltpu.VMEM((nf, mc, BLK, cols), BF16),
        pltpu.VMEM((nf, mc, BLK, cols), BF16),
        pltpu.VMEM((owners * mc, BLK, cols), BF16),
        pltpu.VMEM((gc, BLK, cols), F32),
        pltpu.VMEM((gc, BLK, cols), BF16),
        pltpu.VMEM((nf, gc, BLK, cols), BF16),
        pltpu.VMEM((gc, BLK, cols), F32),
        pltpu.VMEM((nf, gc, 8, BLK), F32),
        pltpu.VMEM((gc, BLK, cols), BF16),
    ]
    scratch += [dma((20 + gc,))]
    for chunks in (1, 1, mc, mc, mc, mc, gc):
        scratch += gather_sems(chunks, mx, subs)
    scratch += [dma((owners + 1,)), dma((owners,))]
    scratch += [dma((owners * mx,))] * 2 + [dma((owners * subs * mx,))] * 2
    scratch += [dma((3 * nf,))] * 2 + [dma((gc * nf,))] * 2
    scratch += [dma((2 * mc,))] * 2 + [dma((mc * (owners + 1),)), dma((mc * owners,))]
    grid_out, mesh_out = pl.pallas_call(
        functools.partial(kernel, (owners, mx, subs)),
        out_shape=(
            jax.ShapeDtypeStruct((gc, BLK, cols), BF16),
            jax.ShapeDtypeStruct((mc, BLK, cols), BF16),
        ),
        in_specs=[smem] * 4 + [hbm] * 19,
        out_specs=(hbm, hbm),
        scratch_shapes=scratch,
        compiler_params=pltpu.CompilerParams(
            collective_id=0, has_side_effects=True, vmem_limit_bytes=62 * 1024 * 1024
        ),
        name="graph_step",
    )(
        enc_src, enc_count, proc_nbr.T, dec_src.T, *(v.reshape(1, cols) for v in vectors), grid_feat,
        mesh_state.reshape(mc, BLK, cols), embed_weight, enc_send_weight, enc_recv_weight,
        enc_out_weight, proc_send_weight, proc_recv_weight, proc_out_weight, dec_send_weight,
        dec_recv_weight, dec_out_weight,
    )
    return grid_out.reshape(gr, cols), mesh_out.reshape(mr, cols)


def solution(mesh):
    rows = P(("groups", "grid"), None)
    both = P(("groups", "grid"), ("mesh", "sub"))
    weight = P(None, ("mesh", "sub"))
    vector = P(("mesh", "sub"))
    return jax.shard_map(
        on_device,
        mesh=mesh,
        in_specs=(
            rows, both, weight, vector, weight, weight, vector, weight, vector, weight, weight,
            vector, weight, vector, weight, weight, vector, weight, vector,
            P("groups", None), P("groups"), P("groups", None), P("groups", None),
        ),
        out_specs=(both, both),
        check_vma=False,
    )
```

```python
import functools

import jax
import jax.numpy as jnp
from jax import lax
from jax.experimental import pallas as pl
from jax.experimental.pallas import tpu as pltpu
from jax.sharding import PartitionSpec as P

BLK = 128
EPSILON = 1e-05
MESH_ID = pl.DeviceIdType.MESH
F32 = jnp.float32
BF16 = jnp.bfloat16
SUBROWS = 32


class Drain:
    def __init__(self):
        self.sent = []

    def send(self, src, dst, send_sem, recv_sem, device):
        copy = pltpu.make_async_remote_copy(
            src_ref=src, dst_ref=dst, send_sem=send_sem, recv_sem=recv_sem,
            device_id=device, device_id_type=MESH_ID,
        )
        copy.start()
        self.sent.append((None, copy))

    def send_if(self, wanted, src, dst, send_sem, recv_sem, device):
        copy = pltpu.make_async_remote_copy(
            src_ref=src, dst_ref=dst, send_sem=send_sem, recv_sem=recv_sem,
            device_id=device, device_id_type=MESH_ID,
        )

        @pl.when(wanted)
        def _():
            copy.start()

        self.sent.append((wanted, copy))

    def arrived(self, dst, send_sem, recv_sem, device):
        pltpu.make_async_remote_copy(
            src_ref=dst, dst_ref=dst, send_sem=send_sem, recv_sem=recv_sem,
            device_id=device, device_id_type=MESH_ID,
        ).wait_recv()

    def finish(self):
        for wanted, copy in self.sent:
            if wanted is None:
                copy.wait_send()
            else:

                @pl.when(wanted)
                def _(copy=copy):
                    copy.wait_send()


class Gather:
    def __init__(self, drain, sizes, place, view, sems, chunks):
        self.drain, self.view = drain, view
        self.xs, self.xr, self.ss, self.sr = sems
        self.mx, self.subs = sizes
        self.m, self.s = place
        self.chunks = chunks

    def shard(self, j, t):
        return lax.rem(self.m + self.mx - j, self.mx) * self.subs + lax.rem(
            self.s + self.subs - t, self.subs
        )

    def xi(self, c, j):
        return c * self.mx + j

    def si(self, c, t, j):
        return (c * self.subs + t) * self.mx + j

    def sib(self, t):
        return {"sub": lax.rem(self.s + t, self.subs)}

    def peer(self, j):
        return {"mesh": lax.rem(self.m + j, self.mx)}

    def issue(self, c, src=None):
        mine = self.view(self.shard(0, 0), c)
        src = mine if src is None else src
        for j in range(1, self.mx):
            i = self.xi(c, j)
            self.drain.send(src, mine, self.xs.at[i], self.xr.at[i], self.peer(j))
        for t in range(1, self.subs):
            i = self.si(c, t, 0)
            self.drain.send(src, mine, self.ss.at[i], self.sr.at[i], self.sib(t))

    def forward(self, c):
        for j in range(1, self.mx):
            i = self.xi(c, j)
            ref = self.view(self.shard(j, 0), c)
            self.drain.arrived(ref, self.xs.at[i], self.xr.at[i], self.peer(j))
            for t in range(1, self.subs):
                k = self.si(c, t, j)
                self.drain.send(ref, ref, self.ss.at[k], self.sr.at[k], self.sib(t))

    def finish(self, c):
        for t in range(1, self.subs):
            for j in range(self.mx):
                k = self.si(c, t, j)
                self.drain.arrived(
                    self.view(self.shard(j, t), c), self.ss.at[k], self.sr.at[k], self.sib(t)
                )


class Line:
    def __init__(self, drain, owners, o, view, sems):
        self.drain, self.owners, self.o, self.view = drain, owners, o, view
        self.ss, self.rs = sems

    def source(self, i):
        tables = [
            sorted((x for x in range(self.owners) if x != r), key=lambda x: (abs(r - x), x))
            for r in range(self.owners)
        ]
        found = jnp.int32(tables[0][i])
        for r in range(1, self.owners):
            found = jnp.where(self.o == r, jnp.int32(tables[r][i]), found)
        return found

    def issue(self, c, src=None):
        mine = self.view(self.o, c)
        src = mine if src is None else src
        arrive = self.rs.at[c * self.owners + self.o]
        base = c * (self.owners + 1)
        last = self.owners - 1
        right = {"grid": jnp.minimum(self.o + 1, last)}
        left = {"grid": jnp.maximum(self.o - 1, 0)}
        self.drain.send_if(self.o < last, src, mine, self.ss.at[base + self.o], arrive, right)
        self.drain.send_if(self.o > 0, src, mine, self.ss.at[base + self.owners], arrive, left)

    def receive(self, source, c):
        ref = self.view(source, c)
        arrive = self.rs.at[c * self.owners + source]
        sent = self.ss.at[c * (self.owners + 1) + source]
        last = self.owners - 1
        onward = jnp.where(source < self.o, self.o + 1, self.o - 1)
        device = {"grid": jnp.clip(onward, 0, last)}
        self.drain.arrived(ref, sent, arrive, device)
        self.drain.send_if((onward >= 0) & (onward <= last), ref, ref, sent, arrive, device)


def gather_sems(chunks, mx, subs):
    return [pltpu.SemaphoreType.DMA((chunks * mx,))] * 2 + [
        pltpu.SemaphoreType.DMA((chunks * subs * mx,))
    ] * 2


def edges(target, receiver, bias_free, sources):
    @pl.loop(0, BLK // SUBROWS)
    def _(r):
        rows = pl.ds(pl.multiple_of(r * SUBROWS, SUBROWS), SUBROWS)
        base = receiver(rows)
        total = bias_free(rows)
        for load, weight in sources:
            half = load(rows).astype(F32) + base
            active = half + half * jnp.tanh(half)
            if weight is not None:
                active = active * weight
            total = active if total is None else total + active
        target(rows, total)


def kernel(
    sizes, enc_src, enc_count, proc_nbr, dec_src, e_gain, c_gain, p_gain, d_gain,
    e_bias, p_bias, d_bias, grid_feat, mesh_state, embed_w,
    es_w, er_w, eo_w, ps_w, pr_w, po_w, ds_w, dr_w, do_w,
    grid_out, mesh_out,
    w_es, w_er, w_eo, w_ps, w_pr, w_po, w_ds, w_dr, w_do,
    we_all, gains, local, ms_all, feats, wec, m_enc, m_dec, enc_all, enc_recv,
    hid1, out1, mid_all, win, proc_recv, hid2, out2, mo_all, dsend, dec_recv, gstate,
    hid3, dec_out, stats, g_stage,
    lsem,
    we_xs, we_xr, we_ss, we_sr,
    ms_xs, ms_xr, ms_ss, ms_sr,
    h1_xs, h1_xr, h1_ss, h1_sr,
    o1_xs, o1_xr, o1_ss, o1_sr,
    h2_xs, h2_xr, h2_ss, h2_sr,
    o2_xs, o2_xr, o2_ss, o2_sr,
    h3_xs, h3_xr, h3_ss, h3_sr,
    fz_s, fz_r, fx_s, fx_r, fs_s, fs_r,
    pp_s, pp_r, st_s, st_r, wz_s, wz_r, dz_s, dz_r,
):
    owners, mx, subs = sizes
    nf = mx * subs
    o, m, s = lax.axis_index("grid"), lax.axis_index("mesh"), lax.axis_index("sub")
    f_me = m * subs + s
    mc = mesh_state.shape[0]
    cols = mesh_state.shape[2]
    gr, fin = grid_feat.shape
    gc = gr // BLK
    d_all = nf * cols
    part = gr // nf
    drain = Drain()

    loads = []

    def load(src, dst):
        copy = pltpu.make_async_copy(src, dst, lsem.at[len(loads)])
        copy.start()
        loads.append(copy)
        return copy

    l_we = load(embed_w, we_all.at[f_me])
    gain_refs = (e_gain, c_gain, p_gain)
    l_small = [load(ref, gains.at[k, f_me]) for k, ref in enumerate(gain_refs)]
    l_small += [load(ref, local.at[k]) for k, ref in enumerate((d_gain, e_bias, p_bias, d_bias))]
    feature_peers = []
    for j in range(mx):
        for t in range(subs):
            if j or t:
                feature_peers.append(
                    {"mesh": lax.rem(m + j, mx), "sub": lax.rem(s + t, subs)}
                )
    left, right = {"grid": lax.rem(o + owners - 1, owners)}, {"grid": lax.rem(o + 1, owners)}
    grid_peers = [left, right]
    barrier = pltpu.get_barrier_semaphore()
    for device in feature_peers + grid_peers:
        pl.semaphore_signal(barrier, inc=1, device_id=device, device_id_type=MESH_ID)
    pl.semaphore_wait(barrier, len(feature_peers) + len(grid_peers))

    def gather(view, sems, chunks):
        return Gather(drain, (mx, subs), (m, s), view, sems, chunks)

    g_we = gather(lambda f, c: we_all.at[f], (we_xs, we_xr, we_ss, we_sr), 1)
    g_ms = gather(lambda f, c: ms_all.at[f], (ms_xs, ms_xr, ms_ss, ms_sr), 1)
    block_view = lambda buf: (lambda f, c: buf.at[f, c])
    g_h1 = gather(block_view(hid1), (h1_xs, h1_xr, h1_ss, h1_sr), mc)
    g_o1 = gather(block_view(out1), (o1_xs, o1_xr, o1_ss, o1_sr), mc)
    g_h2 = gather(block_view(hid2), (h2_xs, h2_xr, h2_ss, h2_sr), mc)
    g_o2 = gather(block_view(out2), (o2_xs, o2_xr, o2_ss, o2_sr), mc)
    g_h3 = gather(block_view(hid3), (h3_xs, h3_xr, h3_ss, h3_sr), gc)

    def peer_shard(p):
        j, t = (p + 1) // subs, (p + 1) % subs
        return lax.rem(m + mx - j, mx) * subs + lax.rem(s + subs - t, subs)

    g_we.issue(0, embed_w)
    for p, device in enumerate(feature_peers):
        for k, ref in enumerate(gain_refs):
            i = k * nf + p
            drain.send(ref, gains.at[k, f_me], pp_s.at[i], pp_r.at[i], device)

    def part_rows(f):
        return pl.ds(pl.multiple_of(f * part, part), part)

    z_feat = Line(drain, owners, o, lambda c, _: feats.at[c, part_rows(f_me)], (fz_s, fz_r))
    z_feat.issue(0, grid_feat.at[part_rows(f_me)])
    g_ms.issue(0, mesh_state)
    l_es = load(es_w, w_es)
    l_dr = load(dr_w, w_dr)
    l_feat = load(grid_feat, feats.at[o])
    l_ms = load(mesh_state, ms_all.at[f_me])
    l_er, l_eo, l_ps, l_pr, l_po, l_ds, l_do = (
        load(a, b)
        for a, b in (
            (er_w, w_er), (eo_w, w_eo), (ps_w, w_ps), (pr_w, w_pr), (po_w, w_po), (ds_w, w_ds),
            (do_w, w_do),
        )
    )
    g_feat = gather(lambda f, c: feats.at[c, part_rows(f)], (fx_s, fx_r, fs_s, fs_r), owners)
    others = [z_feat.source(i) for i in range(owners - 1)]

    g_we.forward(0)
    l_we.wait()
    g_we.finish(0)
    for copy in l_small:
        copy.wait()
    for p, device in enumerate(feature_peers):
        for k in range(len(gain_refs)):
            i = k * nf + p
            drain.arrived(gains.at[k, peer_shard(p)], pp_s.at[i], pp_r.at[i], device)
    l_es.wait()
    l_dr.wait()

    row_sum = None
    for f in range(nf):
        one = jnp.sum(we_all[f].astype(F32), axis=1, keepdims=True)
        row_sum = one if row_sum is None else row_sum + one
    row_mean = row_sum / d_all
    enc_map = dec_map = None
    for f in range(nf):
        centred = we_all[f].astype(F32) - row_mean
        wec[f] = centred.astype(BF16)
        gained = (centred * gains[0, f]).astype(BF16)
        a = jnp.dot(gained, w_es[f * cols : (f + 1) * cols, :], preferred_element_type=F32)
        b = jnp.dot(gained, w_dr[f * cols : (f + 1) * cols, :], preferred_element_type=F32)
        enc_map = a if enc_map is None else enc_map + a
        dec_map = b if dec_map is None else dec_map + b
    m_enc[...] = (0.5 * enc_map).astype(BF16)
    m_dec[...] = (0.5 * dec_map).astype(BF16)

    pair = 2 if gc % 2 == 0 else 1

    def project(owner, own):
        @pl.loop(0, gc // pair)
        def _(i):
            rows = pl.ds(pl.multiple_of(i * (pair * BLK), pair * BLK), pair * BLK)
            x = feats[owner, rows, :]
            squares = None
            for f in range(nf):
                v = jnp.dot(x, wec[f], preferred_element_type=F32)
                one = jnp.sum(v * v, axis=1, keepdims=True)
                squares = one if squares is None else squares + one
            scale = lax.rsqrt(squares / d_all + EPSILON)
            sent = jnp.dot(x, m_enc[...], preferred_element_type=F32) * scale
            blocks = pl.ds(owner * gc + i * pair, pair)
            enc_all[blocks] = sent.reshape(pair, BLK, cols)
            if own:
                got = jnp.dot(x, m_dec[...], preferred_element_type=F32) * scale
                got = got + 0.5 * local[3]
                dec_recv[pl.ds(i * pair, pair)] = got.reshape(pair, BLK, cols)
                state = jnp.dot(x, wec[f_me], preferred_element_type=F32) * scale
                state = (state * gains[0, f_me]).astype(BF16)
                gstate[pl.ds(i * pair, pair)] = state.reshape(pair, BLK, cols)

    l_feat.wait()

    def take(source):
        z_feat.receive(source, 0)
        g_feat.issue(source)

    for source in others[:-1]:
        take(source)
    project(o, True)
    take(others[-1])
    g_ms.forward(0)
    for source in others[:-1]:
        g_feat.forward(source)
    l_ms.wait()
    g_ms.finish(0)
    l_er.wait()

    def product(buf, b, weight):
        total = None
        for f in range(nf):
            one = jnp.dot(buf[f, b], weight[f * cols : (f + 1) * cols, :], preferred_element_type=F32)
            total = one if total is None else total + one
        return total

    for b in range(mc):
        enc_recv[b] = 0.5 * (product(ms_all, b, w_er) + local[1])
    for i, source in enumerate(others):
        if i == len(others) - 1:
            g_feat.forward(source)
        g_feat.finish(source)
        project(source, False)

    fan = enc_src.shape[1]
    for b in range(mc):
        row = o * mc + b
        count = enc_count[row]
        sources = []
        for k in range(fan):
            idx = jnp.clip(enc_src[row, k], 0, owners * gc - 1)
            weight = jnp.where(k < count, 1.0, 0.0).astype(F32)
            sources.append((lambda rows, idx=idx: enc_all[idx, rows, :], weight))

        def put(rows, value, b=b):
            hid1[f_me, b, rows, :] = value.astype(BF16)

        edges(put, lambda rows, b=b: enc_recv[b, rows, :], lambda rows: None, sources)
        g_h1.issue(b)

    def node_layer(g_h, hid, weight, g_o, out):
        g_h.forward(0)
        for b in range(mc):
            if b + 1 < mc:
                g_h.forward(b + 1)
            g_h.finish(b)
            out[f_me, b] = product(hid, b, weight).astype(BF16)
            g_o.issue(b)
        g_o.forward(0)

    def norm_rows(out, old, new, b, gain_row):
        @pl.loop(0, BLK // SUBROWS)
        def _(r):
            rows = pl.ds(pl.multiple_of(r * SUBROWS, SUBROWS), SUBROWS)
            total = None
            for f in range(nf):
                one = jnp.sum(out[f, b, rows, :].astype(F32), axis=1, keepdims=True)
                total = one if total is None else total + one
            mean = total / d_all
            squares = None
            for f in range(nf):
                c = out[f, b, rows, :].astype(F32) - mean
                one = jnp.sum(c * c, axis=1, keepdims=True)
                squares = one if squares is None else squares + one
            scale = lax.rsqrt(squares / d_all + EPSILON)
            for f in range(nf):
                c = out[f, b, rows, :].astype(F32) - mean
                value = c * scale * gains[gain_row, f]
                new[f, b, rows, :] = (old[f, b, rows, :].astype(F32) + value).astype(BF16)

    l_eo.wait()
    node_layer(g_h1, hid1, w_eo, g_o1, out1)
    l_ps.wait()
    l_pr.wait()
    for b in range(mc):
        if b + 1 < mc:
            g_o1.forward(b + 1)
        g_o1.finish(b)
        norm_rows(out1, ms_all, mid_all, b, 1)
        win[1, b] = (0.5 * product(mid_all, b, w_ps)).astype(BF16)
        drain.send(win.at[1, b], win.at[2, b], wz_s.at[2 * b], wz_r.at[2 * b], left)
        drain.send(win.at[1, b], win.at[0, b], wz_s.at[2 * b + 1], wz_r.at[2 * b + 1], right)
    for b in range(mc):
        proc_recv[b] = 0.5 * (product(mid_all, b, w_pr) + local[2])
    for b in range(mc):
        drain.arrived(win.at[2, b], wz_s.at[2 * b], wz_r.at[2 * b], left)
        drain.arrived(win.at[0, b], wz_s.at[2 * b + 1], wz_r.at[2 * b + 1], right)
    fan = proc_nbr.shape[0]
    for b in range(mc):
        row = o * mc + b
        sources = []
        for q in range(fan):
            side = q * 3 // fan
            home = lax.rem(o + side - 1 + owners, owners)
            idx = jnp.clip(proc_nbr[q, row] - home * mc, 0, mc - 1)
            sources.append((lambda rows, idx=idx, side=side: win[side, idx, rows, :], None))

        def put(rows, value, b=b):
            hid2[f_me, b, rows, :] = value.astype(BF16)

        edges(put, lambda rows, b=b: proc_recv[b, rows, :], lambda rows: None, sources)
        g_h2.issue(b)
    l_po.wait()
    node_layer(g_h2, hid2, w_po, g_o2, out2)
    l_ds.wait()
    z_dec = Line(drain, owners, o, lambda c, b: dsend.at[c * mc + b], (dz_s, dz_r))
    for b in range(mc):
        if b + 1 < mc:
            g_o2.forward(b + 1)
        g_o2.finish(b)
        norm_rows(out2, mid_all, mo_all, b, 2)
        dsend[o * mc + b] = (0.5 * product(mo_all, b, w_ds)).astype(BF16)
        z_dec.issue(b)
    l_out = load(mo_all.at[f_me], mesh_out)
    for source in others:
        for b in range(mc):
            z_dec.receive(source, b)

    fan = dec_src.shape[0]
    for g in range(gc):
        sources = []
        for e in range(fan):
            idx = jnp.clip(dec_src[e, o * gc + g], 0, owners * mc - 1)
            sources.append((lambda rows, idx=idx: dsend[idx, rows, :], None))

        def put(rows, value, g=g):
            hid3[f_me, g, rows, :] = value.astype(BF16)

        edges(put, lambda rows, g=g: dec_recv[g, rows, :], lambda rows: None, sources)
        g_h3.issue(g)

    l_do.wait()
    eye = lax.broadcasted_iota(jnp.int32, (BLK, BLK), 0) == lax.broadcasted_iota(
        jnp.int32, (BLK, BLK), 1
    )

    top = lax.broadcasted_iota(jnp.int32, (8, BLK), 0) == 0

    def to_row(column):
        return jnp.sum(jnp.where(eye, column, 0.0), axis=0, keepdims=True)

    def to_column(row):
        return jnp.sum(jnp.where(eye, row, 0.0), axis=1, keepdims=True)

    def decode(g):
        g_h3.finish(g)
        value = product(hid3, g, w_do)
        dec_out[g] = value
        sums = to_row(jnp.sum(value, axis=1, keepdims=True))
        squares = to_row(jnp.sum(value * value, axis=1, keepdims=True))
        stats[f_me, g] = jnp.where(top, sums, squares)
        for p, device in enumerate(feature_peers):
            i = g * nf + p
            drain.send(stats.at[f_me, g], stats.at[f_me, g], st_s.at[i], st_r.at[i], device)

    outs = []

    def complete(g):
        for p, device in enumerate(feature_peers):
            i = g * nf + p
            drain.arrived(stats.at[peer_shard(p), g], st_s.at[i], st_r.at[i], device)
        total, squares = stats[0, g, 0:1, :], stats[0, g, 1:2, :]
        for f in range(1, nf):
            total = total + stats[f, g, 0:1, :]
            squares = squares + stats[f, g, 1:2, :]
        mean = total / d_all
        scale = lax.rsqrt(squares / d_all - mean * mean + EPSILON)
        value = (dec_out[g] - to_column(mean)) * to_column(scale) * local[0]
        g_stage[g] = (gstate[g].astype(F32) + value).astype(BF16)
        outs.append(load(g_stage.at[g], grid_out.at[g]))

    for g in range(gc):
        g_h3.forward(g)
        if g >= 1:
            decode(g - 1)
    decode(gc - 1)
    for g in range(gc):
        complete(g)
    l_out.wait()
    for copy in outs:
        copy.wait()
    drain.finish()


def on_device(
    grid_feat, mesh_state, embed_weight, embed_gain, enc_send_weight, enc_recv_weight, enc_bias,
    enc_out_weight, enc_gain, proc_send_weight, proc_recv_weight, proc_bias, proc_out_weight,
    proc_gain, dec_send_weight, dec_recv_weight, dec_bias, dec_out_weight, dec_gain,
    enc_src, enc_count, proc_nbr, dec_src,
):
    owners, mx, subs = (lax.axis_size(a) for a in ("grid", "mesh", "sub"))
    nf = mx * subs
    mr, cols = mesh_state.shape
    gr, fin = grid_feat.shape
    mc, gc = mr // BLK, gr // BLK
    depth = enc_send_weight.shape[0]
    vectors = (embed_gain, enc_gain, proc_gain, dec_gain, enc_bias, proc_bias, dec_bias)
    smem = pl.BlockSpec(memory_space=pltpu.SMEM)
    hbm = pl.BlockSpec(memory_space=pl.ANY)
    dma = pltpu.SemaphoreType.DMA
    scratch = [pltpu.VMEM((depth, cols), BF16)] * 9
    scratch += [
        pltpu.VMEM((nf, fin, cols), BF16),
        pltpu.VMEM((3, nf, 1, cols), F32),
        pltpu.VMEM((4, 1, cols), F32),
        pltpu.VMEM((nf, mc, BLK, cols), BF16),
        pltpu.VMEM((owners, gr, fin), BF16),
        pltpu.VMEM((nf, fin, cols), BF16),
        pltpu.VMEM((fin, cols), BF16),
        pltpu.VMEM((fin, cols), BF16),
        pltpu.VMEM((owners * gc, BLK, cols), F32),
        pltpu.VMEM((mc, BLK, cols), F32),
        pltpu.VMEM((nf, mc, BLK, cols), BF16),
        pltpu.VMEM((nf, mc, BLK, cols), BF16),
        pltpu.VMEM((nf, mc, BLK, cols), BF16),
        pltpu.VMEM((3, mc, BLK, cols), BF16),
        pltpu.VMEM((mc, BLK, cols), F32),
        pltpu.VMEM((nf, mc, BLK, cols), BF16),
        pltpu.VMEM((nf, mc, BLK, cols), BF16),
        pltpu.VMEM((nf, mc, BLK, cols), BF16),
        pltpu.VMEM((owners * mc, BLK, cols), BF16),
        pltpu.VMEM((gc, BLK, cols), F32),
        pltpu.VMEM((gc, BLK, cols), BF16),
        pltpu.VMEM((nf, gc, BLK, cols), BF16),
        pltpu.VMEM((gc, BLK, cols), F32),
        pltpu.VMEM((nf, gc, 8, BLK), F32),
        pltpu.VMEM((gc, BLK, cols), BF16),
    ]
    scratch += [dma((20 + gc,))]
    for chunks in (1, 1, mc, mc, mc, mc, gc):
        scratch += gather_sems(chunks, mx, subs)
    scratch += [dma((owners + 1,)), dma((owners,))]
    scratch += [dma((owners * mx,))] * 2 + [dma((owners * subs * mx,))] * 2
    scratch += [dma((3 * nf,))] * 2 + [dma((gc * nf,))] * 2
    scratch += [dma((2 * mc,))] * 2 + [dma((mc * (owners + 1),)), dma((mc * owners,))]
    grid_out, mesh_out = pl.pallas_call(
        functools.partial(kernel, (owners, mx, subs)),
        out_shape=(
            jax.ShapeDtypeStruct((gc, BLK, cols), BF16),
            jax.ShapeDtypeStruct((mc, BLK, cols), BF16),
        ),
        in_specs=[smem] * 4 + [hbm] * 19,
        out_specs=(hbm, hbm),
        scratch_shapes=scratch,
        compiler_params=pltpu.CompilerParams(
            collective_id=0, has_side_effects=True, vmem_limit_bytes=62 * 1024 * 1024
        ),
        name="graph_step",
    )(
        enc_src, enc_count, proc_nbr.T, dec_src.T, *(v.reshape(1, cols) for v in vectors), grid_feat,
        mesh_state.reshape(mc, BLK, cols), embed_weight, enc_send_weight, enc_recv_weight,
        enc_out_weight, proc_send_weight, proc_recv_weight, proc_out_weight, dec_send_weight,
        dec_recv_weight, dec_out_weight,
    )
    return grid_out.reshape(gr, cols), mesh_out.reshape(mr, cols)


def solution(mesh):
    rows = P(("groups", "grid"), None)
    both = P(("groups", "grid"), ("mesh", "sub"))
    weight = P(None, ("mesh", "sub"))
    vector = P(("mesh", "sub"))
    return jax.shard_map(
        on_device,
        mesh=mesh,
        in_specs=(
            rows, both, weight, vector, weight, weight, vector, weight, vector, weight, weight,
            vector, weight, vector, weight, weight, vector, weight, vector,
            P("groups", None), P("groups"), P("groups", None), P("groups", None),
        ),
        out_specs=(both, both),
        check_vma=False,
    )
```
